32 devices in a mesh: tile: 8 (over y, x, core), depth: 4 (over z).
Axes of the slice: x: 2, y: 2, z: 4, core: 2. Of those that a mesh axis runs over, the one named last changes fastest.
Arguments:
- transmission: float32 [2, 4, 1024, 512], P(None, 'depth', 'tile'), may hold values from -1.2 to 1.2, as said below
- probe_wave: float32 [2, 128, 128], replicated, may hold values from -6 to 6
- fresnel_phase: float32 [128, 128], replicated, may hold values from -3.140625 to 3.140625
- measured: float32 [32, 128, 128], P('tile'), may hold values from 0.1 to 4
- positions: int32 [32, 2], P('tile'), may hold values from 0 to 1023, as said below
- extents: int32 [8, 2], P('tile'), may hold values from 32 to 64
Outputs:
- object_grad: float32 [2, 4, 1024, 512], P(None, 'depth', 'tile')
The draws below stay inside these ranges and needn't reach their ends.
Inputs may be any that keep to these rules, and one draw needn't show every extreme that they name: `transmission`: real and imaginary parts of a pixel form a complex number of modulus 0.7 to 1.2. `positions`: probe p belongs to tile t = p // 4. Its first row r satisfies ((r - 128 t + 64) mod 1024) - 64 between -64 and 64, both ends reached in every draw; its first column lies between 0 and 384.
All inputs are finite; a program needn't handle non-finite values.
Results may differ from the reference program's by a relative error of at most 0.025.
Values may be sent and summed in bfloat16 or wider, within the bound.
No kernel may reach another device: no remote copies, remote signals or barrier semaphores. Data moves between devices by JAX's collectives and lax.ppermute only.
A program may use at most 64 MiB of HBM per device.

```python
import math
import jax
import jax.numpy as jnp
from jax import lax

W = 128
BAND = 64
PPT = 4
SL = 1
STRIP = 128
OW = 512
NROWS = 1024
PROBES = 32
SLICES = 4
N_TILE = 8


def draw_transmission(key, part):
    key_amp, key_phase = jax.random.split(jax.random.fold_in(key, 11))
    shape = (SLICES, NROWS, OW)
    amplitude = jax.random.uniform(key_amp, shape, jnp.float32, 0.7, 1.1)
    phase = jax.random.uniform(key_phase, shape, jnp.float32, -1.0, 1.0)
    return jnp.stack([amplitude * jnp.cos(phase), amplitude * jnp.sin(phase)]).astype(jnp.float32)


def draw_positions(key, part):
    key_rows, key_cols, key_first, key_second = jax.random.split(jax.random.fold_in(key, 23), 4)
    probe_ids = jnp.arange(PROBES, dtype=jnp.int32)
    tile_ids = probe_ids // PPT
    offset = jax.random.randint(key_rows, (PROBES,), -BAND, STRIP + BAND - W + 1, dtype=jnp.int32)
    upper_tile = jax.random.randint(key_first, (), 0, N_TILE, dtype=jnp.int32)
    lower_tile = jax.random.randint(key_second, (), 0, N_TILE, dtype=jnp.int32)
    offset = jnp.where(probe_ids == upper_tile * PPT, -BAND, offset)
    offset = jnp.where(probe_ids == lower_tile * PPT + 1, STRIP + BAND - W, offset)
    rows = (tile_ids * STRIP + offset) % NROWS
    columns = jax.random.randint(key_cols, (PROBES,), 0, OW - W + 1, dtype=jnp.int32)
    return jnp.stack([rows, columns], axis=1).astype(jnp.int32)


def set_ends(drawn, rng, least, largest):
    dims = drawn.shape
    place = [jax.random.randint(jax.random.fold_in(rng, axis), (), 0, dims[axis]) for axis in range(len(dims))]
    drawn = drawn.at[tuple(place)].set(least)
    longest = dims.index(max(dims))
    place[longest] = (place[longest] + 1) % dims[longest]
    return drawn.at[tuple(place)].set(largest)


def levels(stream_key, extent, shards, low, top_value):
    def one(dim, parts):
        heights = jax.random.uniform(jax.random.fold_in(jax.random.fold_in(stream_key, 6), dim), (parts,), jnp.float32, low / len(shards), top_value / len(shards))
        return jnp.repeat(jnp.exp(heights), extent[dim] // parts).reshape((-1,) + (1,) * (len(extent) - dim - 1))

    loudness = one(*shards[0])
    for cut in shards[1:]:
        loudness = loudness * one(*cut)
    return loudness


def normal_values(rng, shape, deviation, most, kind=jnp.bfloat16):
    return jnp.clip(deviation * jax.random.normal(rng, shape, jnp.float32), -most, most).astype(kind)


def setup_inputs(seed: int = 0) -> dict:
    arg_keys = jax.random.split(jax.random.key(seed), 7)
    transmission = draw_transmission(jax.random.fold_in(arg_keys[6], 71), 0)
    probe_wave = normal_values(arg_keys[1], (2, W, W), 1.0, 6.0, jnp.float32)
    fresnel_phase = jnp.clip(jax.random.uniform(arg_keys[2], (W, W), jnp.float32, -3.140625, 3.140625), -3.140625, 3.140625)
    measured = jnp.clip(jnp.exp(math.log(4.0) - 3.6888794 * jax.random.uniform(arg_keys[3], (PROBES, W, W), jnp.float32) ** levels(arg_keys[3], (PROBES, W, W), ((0, 8),), -0.2, 0.2)), 0.1, 4.0)
    positions = draw_positions(jax.random.fold_in(arg_keys[6], 71), 0)
    extents = set_ends(jax.random.randint(arg_keys[5], (N_TILE, 2), BAND // 2, BAND + 1), jax.random.fold_in(arg_keys[5], 1), BAND // 2, BAND).astype(jnp.int32)
    return dict(transmission=transmission, probe_wave=probe_wave, fresnel_phase=fresnel_phase, measured=measured, positions=positions, extents=extents)


HIGHEST = lax.Precision.HIGHEST

def tables(length):
    indices = jnp.arange(length, dtype=jnp.int32)
    product = indices[:, None] * indices[None, :] % length
    angles = product.astype(jnp.float32) * (2.0 * math.pi / length)
    factor = 1.0 / math.sqrt(length)
    return (jnp.cos(angles) * factor, jnp.sin(angles) * factor)

def operators(length):
    cosine, sine_table = tables(length)

    def build_pair(direction):
        left_side = jnp.stack([jnp.stack([cosine, direction * sine_table]), jnp.stack([-direction * sine_table, cosine])])
        right_side = jnp.stack([jnp.stack([cosine, -direction * sine_table]), jnp.stack([direction * sine_table, cosine])])
        return (left_side, right_side)
    return (build_pair(1.0), build_pair(-1.0))

def transform(real_part, imag_part, matrices):
    stacked = jnp.stack([real_part, imag_part])
    halfway = jnp.einsum('xyab,ypbc->xpac', matrices[0], stacked, precision=HIGHEST)
    finished = jnp.einsum('ypab,yxbc->xpac', halfway, matrices[1], precision=HIGHEST)
    return (finished[0], finished[1])

def propagate(real_part, imag_part, phase_cos, phase_sin, forward_mats, inverse_mats, conjugate):
    spec_real, spec_imag = transform(real_part, imag_part, forward_mats)
    turned_real = spec_real * phase_cos - conjugate * spec_imag * phase_sin
    turned_imag = spec_imag * phase_cos + conjugate * spec_real * phase_sin
    return transform(turned_real, turned_imag, inverse_mats)

def to_wire(values):
    return lax.optimization_barrier(values.astype(jnp.bfloat16)).astype(jnp.float32)

def reference(transmission, probe_wave, fresnel_phase, measured, positions, extents):
    forward_mats, inverse_mats = operators(W)
    phase_cos = jnp.cos(fresnel_phase)
    phase_sin = jnp.sin(fresnel_phase)
    row_first = positions[:, 0]
    col_first = positions[:, 1]
    probe_ids = jnp.arange(PROBES, dtype=jnp.int32)
    tile_ids = probe_ids // PPT
    offset = (row_first - tile_ids * STRIP + BAND) % NROWS - BAND
    lines = jnp.arange(W, dtype=jnp.int32)
    relative = offset[:, None] + lines[None, :]
    inside = (relative >= -extents[tile_ids, 0][:, None]) & (relative < STRIP + extents[tile_ids, 1][:, None])
    row_mask = inside.astype(jnp.float32)[:, :, None]
    wave_real = probe_wave[0][None] * row_mask
    wave_imag = probe_wave[1][None] * row_mask
    row_index = ((row_first[:, None] + lines[None, :]) % NROWS)[:, :, None]
    col_index = (col_first[:, None] + lines[None, :])[:, None, :]
    waves = []
    layers = []
    for slice_index in range(SLICES):
        layer_real = transmission[0, slice_index][row_index, col_index]
        layer_imag = transmission[1, slice_index][row_index, col_index]
        waves.append((wave_real, wave_imag))
        layers.append((layer_real, layer_imag))
        mixed_real = wave_real * layer_real - wave_imag * layer_imag
        mixed_imag = wave_real * layer_imag + wave_imag * layer_real
        wave_real, wave_imag = propagate(mixed_real, mixed_imag, phase_cos, phase_sin, forward_mats, inverse_mats, 1.0)
        if (slice_index + 1) % SL == 0 and slice_index + 1 < SLICES:
            wave_real = to_wire(wave_real)
            wave_imag = to_wire(wave_imag)
    far_real, far_imag = transform(wave_real, wave_imag, forward_mats)
    misfit = far_real * far_real + far_imag * far_imag - measured
    back_real, back_imag = transform(misfit * far_real, misfit * far_imag, inverse_mats)
    object_grad = jnp.zeros((2, SLICES, NROWS, OW), jnp.float32)
    for slice_index in reversed(range(SLICES)):
        adj_real, adj_imag = propagate(back_real, back_imag, phase_cos, phase_sin, forward_mats, inverse_mats, -1.0)
        held_real, held_imag = waves[slice_index]
        layer_real, layer_imag = layers[slice_index]
        term_real = held_real * adj_real + held_imag * adj_imag
        term_imag = held_real * adj_imag - held_imag * adj_real
        object_grad = object_grad.at[0, slice_index, row_index, col_index].add(term_real)
        object_grad = object_grad.at[1, slice_index, row_index, col_index].add(term_imag)
        back_real = layer_real * adj_real + layer_imag * adj_imag
        back_imag = layer_real * adj_imag - layer_imag * adj_real
        if slice_index % SL == 0 and slice_index > 0:
            back_real = to_wire(back_real)
            back_imag = to_wire(back_imag)
    return object_grad
```

```python
import math

import jax
import jax.numpy as jnp
import numpy as np
from jax import lax
from jax.experimental import pallas as pl
from jax.experimental.pallas import tpu as pltpu
from jax.sharding import PartitionSpec as P

BAND = 64
LANES = 128


SMEM = pl.BlockSpec(memory_space=pltpu.SMEM)
VMEM = pl.BlockSpec(memory_space=pltpu.VMEM)


def tables(length):
    indices = np.arange(length)
    angles = (indices[:, None] * indices[None, :] % length) * (2.0 * math.pi / length)
    cosine, sine = np.cos(angles), np.sin(angles)
    ahead = np.block([[cosine, sine], [-sine, cosine]]).astype(np.float32)
    back = np.block([[cosine, -sine], [sine, cosine]]).astype(np.float32)
    found = []
    for matrix in (ahead, back):
        high = matrix.astype(jnp.bfloat16)
        found += [high, (matrix - high.astype(np.float32)).astype(jnp.bfloat16)]
    return found


def first_row(positions, probe, tile, strip, tiles):
    rows = strip * tiles
    start = positions[probe, 0] - tile * strip + BAND
    start = jnp.where(start < 0, start + rows, start)
    return jnp.where(start >= rows, start - rows, start)


def lanes_of(column):
    block = lax.div(column, LANES)
    return block, column - block * LANES


def cut_kernel(depths, tiles, positions, own, above, below, *refs):
    outs, wide = refs[:-1], refs[-1]
    strip, columns = own.shape[2:]
    window = outs[0].shape[1]
    for block in range(columns // LANES):
        cols = slice(block * LANES, (block + 1) * LANES)
        for part in range(2):
            wide[part, block, :BAND] = above[part, 0, :, cols].astype(jnp.float32)
            wide[part, block, BAND : BAND + strip] = own[part, 0, :, cols]
            wide[part, block, BAND + strip :] = below[part, 0, :, cols].astype(jnp.float32)
    tile, depth = lax.axis_index("tile"), lax.axis_index("depth")
    lane = lax.broadcasted_iota(jnp.int32, (window, LANES), 1)
    for shift, out in enumerate(outs):
        probe = lax.rem(depth + shift, depths)
        row = first_row(positions, probe, tile, strip, tiles)
        block, offset = lanes_of(positions[probe, 1])
        turn = lax.rem(LANES - offset, LANES)
        for part in range(2):
            left = pltpu.roll(wide[part, block, pl.ds(row, window)], turn, 1)
            right = pltpu.roll(wide[part, block + 1, pl.ds(row, window)], turn, 1)
            out[part] = jnp.where(lane < LANES - offset, left, right).astype(out.dtype)


def split(value):
    high = value.astype(jnp.bfloat16)
    return high, (value - high.astype(jnp.float32)).astype(jnp.bfloat16)


def dot(left, right):
    return jnp.dot(left, right, preferred_element_type=jnp.float32)


def from_left(real, imag, matrix, exact):
    half = real.shape[1]
    stacked = jnp.concatenate([real, imag], axis=0)
    if exact:
        high, low = split(stacked)
        both = dot(matrix[0], jnp.concatenate([high, low], axis=1))
        stacked = both[:, :half] + both[:, half:] + dot(matrix[1], high)
    else:
        stacked = dot(matrix[0], stacked.astype(jnp.bfloat16))
    size = real.shape[0]
    return stacked[:size], stacked[size:]


def from_right(real, imag, matrix, exact):
    size = real.shape[0]
    stacked = jnp.concatenate([real, imag], axis=1)
    if exact:
        high, low = split(stacked)
        both = dot(jnp.concatenate([high, low], axis=0), matrix[0])
        stacked = both[:size] + both[size:] + dot(high, matrix[1])
    else:
        stacked = dot(stacked.astype(jnp.bfloat16), matrix[0])
    half = real.shape[1]
    return stacked[:, :half], stacked[:, half:]


def wave_kernel(depths, tiles, strip, positions, extents, probe_wave, phase_cos, phase_sin, measured, *refs):
    matrices, arrived, outs = refs[:4], refs[4 : 4 + depths], refs[4 + depths : 4 + 2 * depths]
    layers, waves = refs[4 + 2 * depths :]
    window = probe_wave.shape[1]
    ahead = [matrices[0][...], matrices[1][...]]
    back = [matrices[2][...], matrices[3][...]]
    tile, depth = lax.axis_index("tile"), lax.axis_index("depth")

    def transform(value, exact):
        return from_right(*from_left(*value, ahead, exact), back, exact)

    def inverse(value, exact):
        return from_right(*from_left(*value, back, exact), ahead, exact)

    for shift in range(depths):
        layers[lax.rem(depth - shift + depths, depths)] = arrived[shift][...].astype(jnp.float32)
    start = first_row(positions, depth, tile, strip, tiles) - BAND
    line = start + lax.broadcasted_iota(jnp.int32, (window, window), 0)
    inside = (line >= -extents[0, 0]) & (line < strip + extents[0, 1])
    real = jnp.where(inside, probe_wave[0], 0.0)
    imag = jnp.where(inside, probe_wave[1], 0.0)
    cosine, sine = phase_cos[...], phase_sin[...]
    scale = 1.0 / window
    for index in range(depths):
        waves[index, 0], waves[index, 1] = real, imag
        layer_real, layer_imag = layers[index, 0], layers[index, 1]
        mixed = (real * layer_real - imag * layer_imag, real * layer_imag + imag * layer_real)
        real, imag = transform(mixed, True)
        if index + 1 < depths:
            turned = (real * cosine - imag * sine, imag * cosine + real * sine)
            real, imag = inverse(turned, True)
    real, imag = real * scale, imag * scale
    misfit = (real * real + imag * imag - measured[0]) * scale
    adjoint = inverse((misfit * real, misfit * imag), False)
    for index in reversed(range(depths)):
        adj_real, adj_imag = adjoint
        held_real, held_imag = waves[index, 0], waves[index, 1]
        waves[index, 0] = held_real * adj_real + held_imag * adj_imag
        waves[index, 1] = held_real * adj_imag - held_imag * adj_real
        if index > 0:
            layer_real, layer_imag = layers[index, 0], layers[index, 1]
            real, imag = transform(
                (layer_real * adj_real + layer_imag * adj_imag, layer_real * adj_imag - layer_imag * adj_real),
                False,
            )
            adjoint = inverse((real * cosine + imag * sine, imag * cosine - real * sine), False)
    for shift in range(depths):
        outs[shift][...] = waves[lax.rem(depth + shift, depths)].astype(jnp.bfloat16)


def add_kernel(depths, tiles, positions, *refs):
    arrived, (own, above, below, wide) = refs[:depths], refs[depths:]
    strip, columns = own.shape[2:]
    window = arrived[0].shape[1]
    tile, depth = lax.axis_index("tile"), lax.axis_index("depth")
    wide[...] = jnp.zeros_like(wide)
    lane = lax.broadcasted_iota(jnp.int32, (window, LANES), 1)
    for shift, value in enumerate(arrived):
        probe = lax.rem(depth - shift + depths, depths)
        rows = pl.ds(first_row(positions, probe, tile, strip, tiles), window)
        block, offset = lanes_of(positions[probe, 1])
        for part in range(2):
            turned = pltpu.roll(value[part].astype(jnp.float32), offset, 1)
            wide[part, block, rows] += jnp.where(lane >= offset, turned, 0.0)
            wide[part, block + 1, rows] += jnp.where(lane < offset, turned, 0.0)
    for block in range(columns // LANES):
        cols = slice(block * LANES, (block + 1) * LANES)
        for part in range(2):
            above[part, 0, :, cols] = wide[part, block, :BAND].astype(jnp.bfloat16)
            own[part, 0, :, cols] = wide[part, block, BAND : BAND + strip]
            below[part, 0, :, cols] = wide[part, block, BAND + strip :].astype(jnp.bfloat16)


def edge_kernel(own, from_prior, from_next, out):
    strip = own.shape[2]
    out[...] = own[...]
    out[:, :, :BAND] += from_prior[...].astype(jnp.float32)
    out[:, :, strip - BAND :] += from_next[...].astype(jnp.float32)


def shards(transmission, probe_wave, fresnel_phase, measured, positions, extents):
    tiles, depths = lax.axis_size("tile"), lax.axis_size("depth")
    strip, columns = transmission.shape[2:]
    window = probe_wave.shape[1]
    assert positions.shape[0] == depths and transmission.shape[1] == 1
    wide = pltpu.VMEM((2, columns // LANES + 1, strip + 2 * BAND, LANES), jnp.float32)
    patch = jax.ShapeDtypeStruct((2, window, window), jnp.bfloat16)

    def along(value, axis, by):
        peers = lax.axis_size(axis)
        return lax.ppermute(value, axis, [(i, (i + by) % peers) for i in range(peers)])

    def spread(values):
        return [along(v, "depth", s) if s else v for s, v in enumerate(values)]

    above = along(transmission[:, :, strip - BAND :].astype(jnp.bfloat16), "tile", 1)
    below = along(transmission[:, :, :BAND].astype(jnp.bfloat16), "tile", -1)
    windows = pl.pallas_call(
        lambda *refs: cut_kernel(depths, tiles, *refs),
        out_shape=[patch] * depths,
        in_specs=[SMEM, VMEM, VMEM, VMEM],
        out_specs=[VMEM] * depths,
        scratch_shapes=[wide],
        name="cut",
    )(positions, transmission, above, below)
    scale = 1.0 / window**2
    phase_cos, phase_sin = jnp.cos(fresnel_phase) * scale, jnp.sin(fresnel_phase) * scale
    mine = lax.dynamic_slice_in_dim(measured, lax.axis_index("depth"), 1, 0)
    pieces = pl.pallas_call(
        lambda *refs: wave_kernel(depths, tiles, strip, *refs),
        out_shape=[patch] * depths,
        in_specs=[SMEM, SMEM] + [VMEM] * (8 + depths),
        out_specs=[VMEM] * depths,
        scratch_shapes=[pltpu.VMEM((depths, 2, window, window), jnp.float32)] * 2,
        name="wave",
    )(positions, extents, probe_wave, phase_cos, phase_sin, mine, *map(jnp.asarray, tables(window)), *spread(windows))
    band = jax.ShapeDtypeStruct((2, 1, BAND, columns), jnp.bfloat16)
    own, top, bottom = pl.pallas_call(
        lambda *refs: add_kernel(depths, tiles, *refs),
        out_shape=[jax.ShapeDtypeStruct(transmission.shape, jnp.float32), band, band],
        in_specs=[SMEM] + [VMEM] * depths,
        out_specs=[VMEM] * 3,
        scratch_shapes=[wide],
        name="add",
    )(positions, *spread(pieces))
    return pl.pallas_call(
        edge_kernel,
        out_shape=jax.ShapeDtypeStruct(transmission.shape, jnp.float32),
        in_specs=[VMEM] * 3,
        out_specs=VMEM,
        name="edge",
    )(own, along(bottom, "tile", 1), along(top, "tile", -1))


def solution(mesh):
    placed = (
        P(None, "depth", "tile", None),
        P(),
        P(),
        P("tile", None, None),
        P("tile", None),
        P("tile", None),
    )
    return jax.shard_map(
        shards,
        mesh=mesh,
        in_specs=placed,
        out_specs=P(None, "depth", "tile", None),
        check_vma=False,
    )
```

```python
import math

import jax
import jax.numpy as jnp
import numpy as np
from jax import lax
from jax.experimental import pallas as pl
from jax.experimental.pallas import tpu as pltpu
from jax.sharding import PartitionSpec as P

BAND = 64
LANES = 128
SPAN = 1 << 16


SMEM = pl.BlockSpec(memory_space=pltpu.SMEM)
VMEM = pl.BlockSpec(memory_space=pltpu.VMEM)
PARAMS = pltpu.CompilerParams(vmem_limit_bytes=12 << 20)


def tables(length):
    indices = np.arange(length)
    angles = (indices[:, None] * indices[None, :] % length) * (2.0 * math.pi / length)
    cosine, sine = np.cos(angles), np.sin(angles)
    ahead = np.block([[cosine, sine], [-sine, cosine]]).astype(np.float32)
    back = np.block([[cosine, -sine], [sine, cosine]]).astype(np.float32)
    found = []
    for matrix in (ahead, back):
        high = matrix.astype(jnp.bfloat16)
        found += [high, (matrix - high.astype(np.float32)).astype(jnp.bfloat16)]
    return found


def first_row(positions, probe, tile, strip, tiles):
    rows = strip * tiles
    start = positions[0, probe] - tile * strip + BAND
    start = jnp.where(start < 0, start + rows, start)
    return jnp.where(start >= rows, start - rows, start)


def placed(codes, place):
    code = codes[place : place + 1, :1][0, 0]
    row = lax.div(code, SPAN)
    column = code - row * SPAN
    block = lax.div(column, LANES)
    return row, block, column - block * LANES


def edge_half(row, strip):
    upper = row < BAND
    return jnp.where(upper, 0, BAND), jnp.where(upper, row, row + strip - BAND)


def turned_pair(wide, part, block, rows, offset, lane):
    turn = lax.rem(LANES - offset, LANES)
    left = pltpu.roll(wide[part, block, rows], turn, 1)
    right = pltpu.roll(wide[part, block + 1, rows], turn, 1)
    return jnp.where(lane < LANES - offset, left, right)


def cut_kernel(order, tiles, positions, extents, own, probe_wave, fresnel_phase, out, codes, incident, turn, wide):
    strip, columns = own.shape[2:]
    window = out.shape[2]
    tile, depth = lax.axis_index("tile"), lax.axis_index("depth")
    for block in range(columns // LANES):
        for part in range(2):
            wide[part, block, BAND : BAND + strip] = own[part, 0, :, block * LANES : (block + 1) * LANES]
    lane = lax.broadcasted_iota(jnp.int32, (window, LANES), 1)
    for place, mask in enumerate(order):
        probe = depth ^ mask
        row, column = first_row(positions, probe, tile, strip, tiles), positions[1, probe]
        codes[place : place + 1] = jnp.full((1, LANES), row * SPAN + column, jnp.int32)
        block = lax.div(column, LANES)
        offset = column - block * LANES
        for part in range(2):
            out[place, part] = turned_pair(wide, part, block, pl.ds(row, window), offset, lane)
    line = first_row(positions, depth, tile, strip, tiles) - BAND + lax.broadcasted_iota(jnp.int32, (window, window), 0)
    inside = (line >= -extents[0, 0]) & (line < strip + extents[0, 1])
    for part in range(2):
        incident[part] = jnp.where(inside, probe_wave[part], 0.0)
    scale = 1.0 / window**2
    turn[0] = jnp.cos(fresnel_phase[...]) * scale
    turn[1] = jnp.sin(fresnel_phase[...]) * scale


def join_kernel(strip, codes, windows, outer, inner, *refs):
    outs, wide = refs[:-1], refs[-1]
    columns = outer.shape[3]
    window = windows.shape[2]
    odd = lax.rem(lax.axis_index("tile"), 2)
    for block in range(columns // LANES):
        cols = slice(block * LANES, (block + 1) * LANES)
        for part in range(2):
            far = pl.multiple_of(odd * (strip + BAND), BAND)
            near = pl.multiple_of((1 - odd) * (strip + BAND), BAND)
            wide[part, block, pl.ds(far, BAND)] = outer[part, 0, :, cols].astype(jnp.float32)
            wide[part, block, pl.ds(near, BAND)] = inner[part, 0, :, cols].astype(jnp.float32)
    lane = lax.broadcasted_iota(jnp.int32, (BAND, LANES), 1)
    line = lax.broadcasted_iota(jnp.int32, (BAND, LANES), 0)
    for place, out in enumerate(outs):
        row, block, offset = placed(codes, place)
        half, start = edge_half(row, strip)
        within = row + half + line
        outside = (within < BAND) | (within >= BAND + strip)
        half = pl.multiple_of(half, BAND)
        other = pl.multiple_of(window - BAND - half, BAND)
        for part in range(2):
            band = turned_pair(wide, part, block, pl.ds(start, BAND), offset, lane)
            mine = windows[place, part, pl.ds(half, BAND)]
            out[part, pl.ds(half, BAND)] = jnp.where(outside, band, mine).astype(jnp.bfloat16)
            out[part, pl.ds(other, BAND)] = windows[place, part, pl.ds(other, BAND)].astype(jnp.bfloat16)


def split(value):
    high = value.astype(jnp.bfloat16)
    return high, (value - high.astype(jnp.float32)).astype(jnp.bfloat16)


def dot(left, right):
    return jnp.dot(left, right, preferred_element_type=jnp.float32)


def from_left(real, imag, matrix, exact):
    half = real.shape[1]
    stacked = jnp.concatenate([real, imag], axis=0)
    if exact:
        high, low = split(stacked)
        both = dot(matrix[0], jnp.concatenate([high, low], axis=1))
        stacked = both[:, :half] + both[:, half:] + dot(matrix[1], high)
    else:
        stacked = dot(matrix[0], stacked.astype(jnp.bfloat16))
    size = real.shape[0]
    return stacked[:size], stacked[size:]


def from_right(real, imag, matrix, exact):
    size = real.shape[0]
    stacked = jnp.concatenate([real, imag], axis=1)
    if exact:
        high, low = split(stacked)
        both = dot(jnp.concatenate([high, low], axis=0), matrix[0])
        stacked = both[:size] + both[size:] + dot(high, matrix[1])
    else:
        stacked = dot(stacked.astype(jnp.bfloat16), matrix[0])
    half = real.shape[1]
    return stacked[:, :half], stacked[:, half:]


def wave_kernel(order, incident, turn, measured, *refs):
    depths = len(order)
    matrices, arrived, outs = refs[:4], refs[4 : 4 + depths], refs[4 + depths : 4 + 2 * depths]
    layers, waves = refs[4 + 2 * depths :]
    window = incident.shape[1]
    ahead = [matrices[0][...], matrices[1][...]]
    back = [matrices[2][...], matrices[3][...]]
    depth = lax.axis_index("depth")

    def transform(value, exact):
        return from_right(*from_left(*value, ahead, exact), back, exact)

    def inverse(value, exact):
        return from_right(*from_left(*value, back, exact), ahead, exact)

    for mask, value in zip(order, arrived):
        layers[depth ^ mask] = value[...].astype(jnp.float32)
    real, imag = incident[0], incident[1]
    cosine, sine = turn[0], turn[1]
    scale = 1.0 / window
    for index in range(depths):
        waves[index, 0], waves[index, 1] = real, imag
        layer_real, layer_imag = layers[index, 0], layers[index, 1]
        mixed = (real * layer_real - imag * layer_imag, real * layer_imag + imag * layer_real)
        real, imag = transform(mixed, True)
        if index + 1 < depths:
            turned = (real * cosine - imag * sine, imag * cosine + real * sine)
            real, imag = inverse(turned, True)
    real, imag = real * scale, imag * scale
    misfit = (real * real + imag * imag - measured[depth]) * scale
    adjoint = inverse((misfit * real, misfit * imag), False)
    for index in reversed(range(depths)):
        adj_real, adj_imag = adjoint
        held_real, held_imag = waves[index, 0], waves[index, 1]
        waves[index, 0] = held_real * adj_real + held_imag * adj_imag
        waves[index, 1] = held_real * adj_imag - held_imag * adj_real
        if index > 0:
            layer_real, layer_imag = layers[index, 0], layers[index, 1]
            real, imag = transform(
                (layer_real * adj_real + layer_imag * adj_imag, layer_real * adj_imag - layer_imag * adj_real),
                False,
            )
            adjoint = inverse((real * cosine + imag * sine, imag * cosine - real * sine), False)
    for mask, out in zip(order, outs):
        out[...] = waves[depth ^ mask].astype(jnp.bfloat16)


def added(wide, part, block, rows, value, offset, lane):
    value = pltpu.roll(value, offset, 1)
    wide[part, block, rows] += jnp.where(lane >= offset, value, 0.0)
    wide[part, block + 1, rows] += jnp.where(lane < offset, value, 0.0)


def shed_kernel(strip, codes, *refs):
    arrived, (outer, inner, wide) = refs[:-3], refs[-3:]
    columns = outer.shape[3]
    odd = lax.rem(lax.axis_index("tile"), 2)
    wide[:, :, :BAND] = jnp.zeros_like(wide[:, :, :BAND])
    wide[:, :, BAND + strip :] = jnp.zeros_like(wide[:, :, :BAND])
    lane = lax.broadcasted_iota(jnp.int32, (BAND, LANES), 1)
    for place, value in enumerate(arrived):
        row, block, offset = placed(codes, place)
        half, start = edge_half(row, strip)
        half = pl.multiple_of(half, BAND)
        for part in range(2):
            piece = value[part, pl.ds(half, BAND)].astype(jnp.float32)
            added(wide, part, block, pl.ds(start, BAND), piece, offset, lane)
    far = pl.multiple_of(odd * (strip + BAND), BAND)
    near = pl.multiple_of((1 - odd) * (strip + BAND), BAND)
    for block in range(columns // LANES):
        cols = slice(block * LANES, (block + 1) * LANES)
        for part in range(2):
            outer[part, 0, :, cols] = wide[part, block, pl.ds(far, BAND)].astype(jnp.bfloat16)
            inner[part, 0, :, cols] = wide[part, block, pl.ds(near, BAND)].astype(jnp.bfloat16)


def add_kernel(codes, *refs):
    arrived, (own, wide) = refs[:-2], refs[-2:]
    strip, columns = own.shape[2:]
    window = arrived[0].shape[1]
    wide[...] = jnp.zeros_like(wide)
    lane = lax.broadcasted_iota(jnp.int32, (window, LANES), 1)
    for place, value in enumerate(arrived):
        row, block, offset = placed(codes, place)
        for part in range(2):
            added(wide, part, block, pl.ds(row, window), value[part].astype(jnp.float32), offset, lane)
    for block in range(columns // LANES):
        for part in range(2):
            own[part, 0, :, block * LANES : (block + 1) * LANES] = wide[part, block, BAND : BAND + strip]


def edge_kernel(own, outer, inner, out):
    strip = own.shape[2]
    odd = lax.rem(lax.axis_index("tile"), 2)
    out[...] = own[...]
    far = pl.multiple_of(odd * (strip - BAND), BAND)
    near = pl.multiple_of((1 - odd) * (strip - BAND), BAND)
    out[:, :, pl.ds(far, BAND)] += outer[...].astype(jnp.float32)
    out[:, :, pl.ds(near, BAND)] += inner[...].astype(jnp.float32)


def call(kernel, name, outs, operands, scratch=(), scalars=0):
    return pl.pallas_call(
        kernel,
        out_shape=outs,
        in_specs=[SMEM] * scalars + [VMEM] * (len(operands) - scalars),
        out_specs=jax.tree.map(lambda _: VMEM, outs),
        scratch_shapes=list(scratch),
        compiler_params=PARAMS,
        name=name,
    )(*operands)


def shards(transmission, probe_wave, fresnel_phase, measured, positions, extents):
    tiles, depths = lax.axis_size("tile"), lax.axis_size("depth")
    strip, columns = transmission.shape[2:]
    window = probe_wave.shape[1]
    assert positions.shape[0] == depths == 4 and transmission.shape[1] == 1 and tiles % 2 == 0
    assert strip == 2 * BAND == window
    order = (2, 3, 1, 0)
    wide = [pltpu.VMEM((2, columns // LANES + 1, strip + 2 * BAND, LANES), jnp.float32)]
    patch = jax.ShapeDtypeStruct((2, window, window), jnp.bfloat16)
    band = jax.ShapeDtypeStruct((2, 1, BAND, columns), jnp.bfloat16)
    odd = lax.axis_index("tile") % 2 == 1

    def swapped(values):
        swaps = [[(d, d ^ mask) for d in range(depths)] for mask in order]
        return [lax.ppermute(v, "depth", swap) if mask else v for v, swap, mask in zip(values, swaps, order)]

    def outward(value):
        return lax.ppermute(value, "tile", [(t, (t - 1 + 2 * (t % 2)) % tiles) for t in range(tiles)])

    def inward(value):
        return lax.ppermute(value, "tile", [(t, t ^ 1) for t in range(tiles)])

    head, tail = transmission[:, :, :BAND], transmission[:, :, strip - BAND :]
    outer = outward(jnp.where(odd, tail, head).astype(jnp.bfloat16))
    inner = inward(jnp.where(odd, head, tail).astype(jnp.bfloat16))
    square = jax.ShapeDtypeStruct((2, window, window), jnp.float32)
    windows, codes, incident, turn = call(
        lambda *refs: cut_kernel(order, tiles, *refs),
        "cut",
        [
            jax.ShapeDtypeStruct((depths, 2, window, window), jnp.float32),
            jax.ShapeDtypeStruct((depths, LANES), jnp.int32),
            square,
            square,
        ],
        [positions.T, extents, transmission, probe_wave, fresnel_phase],
        wide,
        scalars=2,
    )
    windows = call(
        lambda *refs: join_kernel(strip, *refs), "join", [patch] * depths, [codes, windows, outer, inner], wide
    )
    pieces = call(
        lambda *refs: wave_kernel(order, *refs),
        "wave",
        [patch] * depths,
        [incident, turn, measured, *map(jnp.asarray, tables(window)), *swapped(windows)],
        [pltpu.VMEM((depths, 2, window, window), jnp.float32)] * 2,
    )
    pieces = swapped(pieces)
    outer, inner = call(lambda *refs: shed_kernel(strip, *refs), "shed", [band] * 2, [codes, *pieces], wide)
    total = jax.ShapeDtypeStruct(transmission.shape, jnp.float32)
    own = call(add_kernel, "add", total, [codes, *pieces], wide)
    return call(edge_kernel, "edge", total, [own, outward(outer), inward(inner)])


def solution(mesh):
    placed = (
        P(None, "depth", "tile", None),
        P(),
        P(),
        P("tile", None, None),
        P("tile", None),
        P("tile", None),
    )
    return jax.shard_map(
        shards,
        mesh=mesh,
        in_specs=placed,
        out_specs=P(None, "depth", "tile", None),
        check_vma=False,
    )
```

```python
import math

import jax
import jax.numpy as jnp
import numpy as np
from jax import lax
from jax.experimental import pallas as pl
from jax.experimental.pallas import tpu as pltpu
from jax.sharding import PartitionSpec as P

BAND = 64
LANES = 128
SPAN = 1 << 16


SMEM = pl.BlockSpec(memory_space=pltpu.SMEM)
VMEM = pl.BlockSpec(memory_space=pltpu.VMEM)
PARAMS = pltpu.CompilerParams(vmem_limit_bytes=12 << 20)


def tables(length):
    indices = np.arange(length)
    angles = (indices[:, None] * indices[None, :] % length) * (2.0 * math.pi / length)
    cosine, sine = np.cos(angles), np.sin(angles)
    ahead = np.block([[cosine, sine], [-sine, cosine]]).astype(np.float32)
    back = np.block([[cosine, -sine], [sine, cosine]]).astype(np.float32)
    found = []
    for matrix in (ahead, back):
        high = matrix.astype(jnp.bfloat16)
        found += [high, (matrix - high.astype(np.float32)).astype(jnp.bfloat16)]
    return found


def first_row(positions, probe, tile, strip, tiles):
    rows = strip * tiles
    start = positions[0, probe] - tile * strip + BAND
    start = jnp.where(start < 0, start + rows, start)
    return jnp.where(start >= rows, start - rows, start)


def placed(codes, place):
    code = codes[place : place + 1, :1][0, 0]
    row = lax.div(code, SPAN)
    column = code - row * SPAN
    block = lax.div(column, LANES)
    return row, block, column - block * LANES


def edge_half(row, strip):
    upper = row < BAND
    return jnp.where(upper, 0, BAND), jnp.where(upper, row, row + strip - BAND)


def turned_pair(wide, part, block, rows, offset, lane):
    turn = lax.rem(LANES - offset, LANES)
    left = pltpu.roll(wide[part, block, rows], turn, 1)
    right = pltpu.roll(wide[part, block + 1, rows], turn, 1)
    return jnp.where(lane < LANES - offset, left, right)


def cut_kernel(order, tiles, positions, own, out, codes, early, wide):
    strip, columns = own.shape[2:]
    window = out.shape[2]
    tile, depth = lax.axis_index("tile"), lax.axis_index("depth")
    for block in range(columns // LANES):
        for part in range(2):
            wide[part, block, BAND : BAND + strip] = own[part, 0, :, block * LANES : (block + 1) * LANES]
    lane = lax.broadcasted_iota(jnp.int32, (window, LANES), 1)
    for place, mask in enumerate(order):
        probe = depth ^ mask
        row, column = first_row(positions, probe, tile, strip, tiles), positions[1, probe]
        codes[place : place + 1] = jnp.full((1, LANES), row * SPAN + column, jnp.int32)
        block = lax.div(column, LANES)
        offset = column - block * LANES
        for part in range(2):
            out[place, part] = turned_pair(wide, part, block, pl.ds(row, window), offset, lane)
        if place == 0:
            half, _ = edge_half(row, strip)
            other = pl.multiple_of(window - BAND - half, BAND)
            early[...] = out[0, :, pl.ds(other, BAND)].astype(early.dtype)


def prep_kernel(strip, extents, codes, probe_wave, fresnel_phase, incident, turn):
    window = probe_wave.shape[1]
    row, _, _ = placed(codes, codes.shape[0] - 1)
    line = row - BAND + lax.broadcasted_iota(jnp.int32, (window, window), 0)
    inside = (line >= -extents[0, 0]) & (line < strip + extents[0, 1])
    for part in range(2):
        incident[part] = jnp.where(inside, probe_wave[part], 0.0)
    scale = 1.0 / window**2
    turn[0] = jnp.cos(fresnel_phase[...]) * scale
    turn[1] = jnp.sin(fresnel_phase[...]) * scale


def join_kernel(strip, codes, windows, outer, inner, *refs):
    outs, wide = refs[:-1], refs[-1]
    columns = outer.shape[3]
    window = windows.shape[2]
    odd = lax.rem(lax.axis_index("tile"), 2)
    for block in range(columns // LANES):
        cols = slice(block * LANES, (block + 1) * LANES)
        for part in range(2):
            far = pl.multiple_of(odd * (strip + BAND), BAND)
            near = pl.multiple_of((1 - odd) * (strip + BAND), BAND)
            wide[part, block, pl.ds(far, BAND)] = outer[part, 0, :, cols].astype(jnp.float32)
            wide[part, block, pl.ds(near, BAND)] = inner[part, 0, :, cols].astype(jnp.float32)
    lane = lax.broadcasted_iota(jnp.int32, (BAND, LANES), 1)
    line = lax.broadcasted_iota(jnp.int32, (BAND, LANES), 0)
    for place, out in enumerate(outs):
        row, block, offset = placed(codes, place)
        half, start = edge_half(row, strip)
        within = row + half + line
        outside = (within < BAND) | (within >= BAND + strip)
        half = pl.multiple_of(half, BAND)
        other = pl.multiple_of(window - BAND - half, BAND)
        for part in range(2):
            band = turned_pair(wide, part, block, pl.ds(start, BAND), offset, lane)
            joined = jnp.where(outside, band, windows[place, part, pl.ds(half, BAND)]).astype(jnp.bfloat16)
            if place == 0:
                out[part] = joined
                continue
            out[part, pl.ds(half, BAND)] = joined
            out[part, pl.ds(other, BAND)] = windows[place, part, pl.ds(other, BAND)].astype(jnp.bfloat16)


def split(value):
    high = value.astype(jnp.bfloat16)
    return high, (value - high.astype(jnp.float32)).astype(jnp.bfloat16)


def dot(left, right):
    return jnp.dot(left, right, preferred_element_type=jnp.float32)


def from_left(real, imag, matrix, exact):
    half = real.shape[1]
    stacked = jnp.concatenate([real, imag], axis=0)
    if exact:
        high, low = split(stacked)
        both = dot(matrix[0], jnp.concatenate([high, low], axis=1))
        stacked = both[:, :half] + both[:, half:] + dot(matrix[1], high)
    else:
        stacked = dot(matrix[0], stacked.astype(jnp.bfloat16))
    size = real.shape[0]
    return stacked[:size], stacked[size:]


def from_right(real, imag, matrix, exact):
    size = real.shape[0]
    stacked = jnp.concatenate([real, imag], axis=1)
    if exact:
        high, low = split(stacked)
        both = dot(jnp.concatenate([high, low], axis=0), matrix[0])
        stacked = both[:size] + both[size:] + dot(high, matrix[1])
    else:
        stacked = dot(stacked.astype(jnp.bfloat16), matrix[0])
    half = real.shape[1]
    return stacked[:, :half], stacked[:, half:]


def wave_kernel(order, strip, codes, incident, turn, measured, *refs):
    depths = len(order)
    matrices, arrived, outs = refs[:4], refs[4 : 5 + depths], refs[5 + depths : 6 + 2 * depths]
    layers, waves = refs[6 + 2 * depths :]
    window = incident.shape[1]
    ahead = [matrices[0][...], matrices[1][...]]
    back = [matrices[2][...], matrices[3][...]]
    depth = lax.axis_index("depth")

    def transform(value, exact):
        return from_right(*from_left(*value, ahead, exact), back, exact)

    def inverse(value, exact):
        return from_right(*from_left(*value, back, exact), ahead, exact)

    half, _ = edge_half(placed(codes, depths - 1)[0], strip)
    half = pl.multiple_of(half, BAND)
    other = pl.multiple_of(window - BAND - half, BAND)
    for mask, value in zip(order[1:], arrived[2:]):
        layers[depth ^ mask] = value[...].astype(jnp.float32)
    layers[depth ^ order[0], :, pl.ds(half, BAND)] = arrived[0][...].astype(jnp.float32)
    layers[depth ^ order[0], :, pl.ds(other, BAND)] = arrived[1][...].astype(jnp.float32)
    real, imag = incident[0], incident[1]
    cosine, sine = turn[0], turn[1]
    scale = 1.0 / window
    for index in range(depths):
        waves[index, 0], waves[index, 1] = real, imag
        layer_real, layer_imag = layers[index, 0], layers[index, 1]
        mixed = (real * layer_real - imag * layer_imag, real * layer_imag + imag * layer_real)
        real, imag = transform(mixed, True)
        if index + 1 < depths:
            turned = (real * cosine - imag * sine, imag * cosine + real * sine)
            real, imag = inverse(turned, True)
    real, imag = real * scale, imag * scale
    misfit = (real * real + imag * imag - measured[depth]) * scale
    adjoint = inverse((misfit * real, misfit * imag), False)
    for index in reversed(range(depths)):
        adj_real, adj_imag = adjoint
        held_real, held_imag = waves[index, 0], waves[index, 1]
        waves[index, 0] = held_real * adj_real + held_imag * adj_imag
        waves[index, 1] = held_real * adj_imag - held_imag * adj_real
        if index > 0:
            layer_real, layer_imag = layers[index, 0], layers[index, 1]
            real, imag = transform(
                (layer_real * adj_real + layer_imag * adj_imag, layer_real * adj_imag - layer_imag * adj_real),
                False,
            )
            adjoint = inverse((real * cosine + imag * sine, imag * cosine - real * sine), False)
    outs[0][...] = waves[depth ^ order[0], :, pl.ds(half, BAND)].astype(jnp.bfloat16)
    outs[1][...] = waves[depth ^ order[0], :, pl.ds(other, BAND)].astype(jnp.bfloat16)
    for mask, out in zip(order[1:], outs[2:]):
        out[...] = waves[depth ^ mask].astype(jnp.bfloat16)


def added(wide, part, block, rows, value, offset, lane):
    value = pltpu.roll(value, offset, 1)
    wide[part, block, rows] += jnp.where(lane >= offset, value, 0.0)
    wide[part, block + 1, rows] += jnp.where(lane < offset, value, 0.0)


def shed_kernel(strip, codes, *refs):
    arrived, (outer, inner, wide) = refs[:-3], refs[-3:]
    columns = outer.shape[3]
    odd = lax.rem(lax.axis_index("tile"), 2)
    wide[:, :, :BAND] = jnp.zeros_like(wide[:, :, :BAND])
    wide[:, :, BAND + strip :] = jnp.zeros_like(wide[:, :, :BAND])
    lane = lax.broadcasted_iota(jnp.int32, (BAND, LANES), 1)
    for place, value in enumerate(arrived):
        row, block, offset = placed(codes, place)
        half, start = edge_half(row, strip)
        half = pl.multiple_of(half, BAND)
        for part in range(2):
            piece = value[part] if place == 0 else value[part, pl.ds(half, BAND)]
            piece = piece.astype(jnp.float32)
            added(wide, part, block, pl.ds(start, BAND), piece, offset, lane)
    far = pl.multiple_of(odd * (strip + BAND), BAND)
    near = pl.multiple_of((1 - odd) * (strip + BAND), BAND)
    for block in range(columns // LANES):
        cols = slice(block * LANES, (block + 1) * LANES)
        for part in range(2):
            outer[part, 0, :, cols] = wide[part, block, pl.ds(far, BAND)].astype(jnp.bfloat16)
            inner[part, 0, :, cols] = wide[part, block, pl.ds(near, BAND)].astype(jnp.bfloat16)


def add_kernel(codes, early, late, *refs):
    arrived, (own, wide) = refs[:-2], refs[-2:]
    strip, columns = own.shape[2:]
    window = arrived[0].shape[1]
    wide[...] = jnp.zeros_like(wide)
    lane = lax.broadcasted_iota(jnp.int32, (window, LANES), 1)
    row, block, offset = placed(codes, 0)
    half, _ = edge_half(row, strip)
    for value, start in ((early, half), (late, window - BAND - half)):
        for part in range(2):
            piece = value[part].astype(jnp.float32)
            added(wide, part, block, pl.ds(row + start, BAND), piece, offset, lane[:BAND])
    for place, value in enumerate(arrived):
        row, block, offset = placed(codes, place + 1)
        for part in range(2):
            added(wide, part, block, pl.ds(row, window), value[part].astype(jnp.float32), offset, lane)
    for block in range(columns // LANES):
        for part in range(2):
            own[part, 0, :, block * LANES : (block + 1) * LANES] = wide[part, block, BAND : BAND + strip]


def edge_kernel(own, outer, inner, out):
    strip = own.shape[2]
    odd = lax.rem(lax.axis_index("tile"), 2)
    out[...] = own[...]
    far = pl.multiple_of(odd * (strip - BAND), BAND)
    near = pl.multiple_of((1 - odd) * (strip - BAND), BAND)
    out[:, :, pl.ds(far, BAND)] += outer[...].astype(jnp.float32)
    out[:, :, pl.ds(near, BAND)] += inner[...].astype(jnp.float32)


def call(kernel, outs, operands, scratch=(), scalars=0):
    return pl.pallas_call(
        kernel,
        out_shape=outs,
        in_specs=[SMEM] * scalars + [VMEM] * (len(operands) - scalars),
        out_specs=jax.tree.map(lambda _: VMEM, outs),
        scratch_shapes=list(scratch),
        compiler_params=PARAMS,
    )(*operands)


def shards(transmission, probe_wave, fresnel_phase, measured, positions, extents):
    tiles, depths = lax.axis_size("tile"), lax.axis_size("depth")
    strip, columns = transmission.shape[2:]
    window = probe_wave.shape[1]
    assert positions.shape[0] == depths == 4 and transmission.shape[1] == 1 and tiles % 2 == 0
    assert strip == 2 * BAND == window
    order = (2, 3, 1, 0)
    wide = [pltpu.VMEM((2, columns // LANES + 1, strip + 2 * BAND, LANES), jnp.float32)]
    patch = jax.ShapeDtypeStruct((2, window, window), jnp.bfloat16)
    band = jax.ShapeDtypeStruct((2, 1, BAND, columns), jnp.bfloat16)
    odd = lax.axis_index("tile") % 2 == 1

    piece = jax.ShapeDtypeStruct((2, BAND, window), jnp.bfloat16)

    def swap(value, mask):
        if not mask:
            return value
        return lax.ppermute(value, "depth", [(d, d ^ mask) for d in range(depths)])

    def swapped(values):
        return [swap(v, mask) for v, mask in zip(values, order)]

    def outward(value):
        return lax.ppermute(value, "tile", [(t, (t - 1 + 2 * (t % 2)) % tiles) for t in range(tiles)])

    def inward(value):
        return lax.ppermute(value, "tile", [(t, t ^ 1) for t in range(tiles)])

    head, tail = transmission[:, :, :BAND], transmission[:, :, strip - BAND :]
    outer = outward(jnp.where(odd, tail, head).astype(jnp.bfloat16))
    inner = inward(jnp.where(odd, head, tail).astype(jnp.bfloat16))
    square = jax.ShapeDtypeStruct((2, window, window), jnp.float32)
    windows, codes, early = call(
        lambda *refs: cut_kernel(order, tiles, *refs),
        [
            jax.ShapeDtypeStruct((depths, 2, window, window), jnp.float32),
            jax.ShapeDtypeStruct((depths, LANES), jnp.int32),
            piece,
        ],
        [positions.T, transmission],
        wide,
        scalars=1,
    )
    early = swap(early, order[0])
    windows = call(
        lambda *refs: join_kernel(strip, *refs), [piece] + [patch] * (depths - 1), [codes, windows, outer, inner], wide
    )
    probe_wave, fresnel_phase, windows = lax.optimization_barrier((probe_wave, fresnel_phase, windows))
    incident, turn = call(
        lambda *refs: prep_kernel(strip, *refs),
        [square, square],
        [extents, codes, probe_wave, fresnel_phase],
        scalars=1,
    )
    windows = swapped(windows)
    first, late, *pieces = call(
        lambda *refs: wave_kernel(order, strip, *refs),
        [piece] * 2 + [patch] * (depths - 1),
        [codes, incident, turn, measured, *map(jnp.asarray, tables(window)), windows[0], early, *windows[1:]],
        [pltpu.VMEM((depths, 2, window, window), jnp.float32)] * 2,
    )
    first, *pieces = swapped([first, *pieces])
    late = swap(late, order[0])
    outer, inner = call(lambda *refs: shed_kernel(strip, *refs), [band] * 2, [codes, first, *pieces], wide)
    outer, inner = outward(outer), inward(inner)
    total = jax.ShapeDtypeStruct(transmission.shape, jnp.float32)
    own = call(add_kernel, total, [codes, first, late, *pieces], wide)
    return call(edge_kernel, total, [own, outer, inner])


def solution(mesh):
    placed = (
        P(None, "depth", "tile", None),
        P(),
        P(),
        P("tile", None, None),
        P("tile", None),
        P("tile", None),
    )
    return jax.shard_map(
        shards,
        mesh=mesh,
        in_specs=placed,
        out_specs=P(None, "depth", "tile", None),
        check_vma=False,
    )
```

```python
import math

import jax
import jax.numpy as jnp
import numpy as np
from jax import lax
from jax.experimental import pallas as pl
from jax.experimental.pallas import tpu as pltpu
from jax.sharding import PartitionSpec as P

BAND = 64
LANES = 128
SPAN = 1 << 16
ORDER = (2, 3, 1, 0)
EARLY = 2
LATE = 2


SMEM = pl.BlockSpec(memory_space=pltpu.SMEM)
VMEM = pl.BlockSpec(memory_space=pltpu.VMEM)
PARAMS = pltpu.CompilerParams(vmem_limit_bytes=12 << 20)


def tables(length):
    indices = np.arange(length)
    angles = (indices[:, None] * indices[None, :] % length) * (2.0 * math.pi / length)
    cosine, sine = np.cos(angles), np.sin(angles)
    ahead = np.block([[cosine, sine], [-sine, cosine]]).astype(np.float32)
    back = np.block([[cosine, -sine], [sine, cosine]]).astype(np.float32)
    found = []
    for matrix in (ahead, back):
        high = matrix.astype(jnp.bfloat16)
        found += [high, (matrix - high.astype(np.float32)).astype(jnp.bfloat16)]
    return found


def first_row(positions, probe, tile, strip, tiles):
    rows = strip * tiles
    start = positions[0, probe] - tile * strip + BAND
    start = jnp.where(start < 0, start + rows, start)
    return jnp.where(start >= rows, start - rows, start)


def placed(codes, place):
    code = codes[place : place + 1, :1][0, 0]
    row = lax.div(code, SPAN)
    column = code - row * SPAN
    block = lax.div(column, LANES)
    return row, block, column - block * LANES


def edge_half(row, strip):
    upper = row < BAND
    return jnp.where(upper, 0, BAND), jnp.where(upper, row, row + strip - BAND)


def turned_pair(wide, part, block, rows, offset, lane):
    turn = lax.rem(LANES - offset, LANES)
    left = pltpu.roll(wide[part, block, rows], turn, 1)
    right = pltpu.roll(wide[part, block + 1, rows], turn, 1)
    return jnp.where(lane < LANES - offset, left, right)


def cut_kernel(order, tiles, positions, own, out, codes, *refs):
    early, wide = refs[:-1], refs[-1]
    strip, columns = own.shape[2:]
    window = out.shape[2]
    tile, depth = lax.axis_index("tile"), lax.axis_index("depth")
    for block in range(columns // LANES):
        for part in range(2):
            wide[part, block, BAND : BAND + strip] = own[part, 0, :, block * LANES : (block + 1) * LANES]
    lane = lax.broadcasted_iota(jnp.int32, (window, LANES), 1)
    for place, mask in enumerate(order):
        probe = depth ^ mask
        row, column = first_row(positions, probe, tile, strip, tiles), positions[1, probe]
        codes[place : place + 1] = jnp.full((1, LANES), row * SPAN + column, jnp.int32)
        block = lax.div(column, LANES)
        offset = column - block * LANES
        for part in range(2):
            out[place, part] = turned_pair(wide, part, block, pl.ds(row, window), offset, lane)
        if place < len(early):
            half, _ = edge_half(row, strip)
            other = pl.multiple_of(window - BAND - half, BAND)
            early[place][...] = out[place, :, pl.ds(other, BAND)].astype(jnp.bfloat16)


def prep_kernel(strip, extents, codes, probe_wave, fresnel_phase, incident, turn):
    window = probe_wave.shape[1]
    row, _, _ = placed(codes, codes.shape[0] - 1)
    line = row - BAND + lax.broadcasted_iota(jnp.int32, (window, window), 0)
    inside = (line >= -extents[0, 0]) & (line < strip + extents[0, 1])
    for part in range(2):
        incident[part] = jnp.where(inside, probe_wave[part], 0.0)
    scale = 1.0 / window**2
    turn[0] = jnp.cos(fresnel_phase[...]) * scale
    turn[1] = jnp.sin(fresnel_phase[...]) * scale


def join_kernel(strip, codes, windows, outer, inner, *refs):
    outs, wide = refs[:-1], refs[-1]
    columns = outer.shape[3]
    window = windows.shape[2]
    odd = lax.rem(lax.axis_index("tile"), 2)
    for block in range(columns // LANES):
        cols = slice(block * LANES, (block + 1) * LANES)
        for part in range(2):
            far = pl.multiple_of(odd * (strip + BAND), BAND)
            near = pl.multiple_of((1 - odd) * (strip + BAND), BAND)
            wide[part, block, pl.ds(far, BAND)] = outer[part, 0, :, cols].astype(jnp.float32)
            wide[part, block, pl.ds(near, BAND)] = inner[part, 0, :, cols].astype(jnp.float32)
    lane = lax.broadcasted_iota(jnp.int32, (BAND, LANES), 1)
    line = lax.broadcasted_iota(jnp.int32, (BAND, LANES), 0)
    for place, out in enumerate(outs):
        row, block, offset = placed(codes, place)
        half, start = edge_half(row, strip)
        within = row + half + line
        outside = (within < BAND) | (within >= BAND + strip)
        half = pl.multiple_of(half, BAND)
        other = pl.multiple_of(window - BAND - half, BAND)
        for part in range(2):
            band = turned_pair(wide, part, block, pl.ds(start, BAND), offset, lane)
            joined = jnp.where(outside, band, windows[place, part, pl.ds(half, BAND)]).astype(jnp.bfloat16)
            if out.shape[1] == BAND:
                out[part] = joined
                continue
            out[part, pl.ds(half, BAND)] = joined
            out[part, pl.ds(other, BAND)] = windows[place, part, pl.ds(other, BAND)].astype(jnp.bfloat16)


def split(value):
    high = value.astype(jnp.bfloat16)
    return high, (value - high.astype(jnp.float32)).astype(jnp.bfloat16)


def dot(left, right):
    return jnp.dot(left, right, preferred_element_type=jnp.float32)


def from_left(real, imag, matrix, exact):
    half = real.shape[1]
    stacked = jnp.concatenate([real, imag], axis=0)
    if exact:
        high, low = split(stacked)
        both = dot(matrix[0], jnp.concatenate([high, low], axis=1))
        stacked = both[:, :half] + both[:, half:] + dot(matrix[1], high)
    else:
        stacked = dot(matrix[0], stacked.astype(jnp.bfloat16))
    size = real.shape[0]
    return stacked[:size], stacked[size:]


def from_right(real, imag, matrix, exact):
    size = real.shape[0]
    stacked = jnp.concatenate([real, imag], axis=1)
    if exact:
        high, low = split(stacked)
        both = dot(jnp.concatenate([high, low], axis=0), matrix[0])
        stacked = both[:size] + both[size:] + dot(high, matrix[1])
    else:
        stacked = dot(stacked.astype(jnp.bfloat16), matrix[0])
    half = real.shape[1]
    return stacked[:, :half], stacked[:, half:]


def wave_kernel(order, strip, codes, incident, turn, measured, *refs):
    depths = len(order)
    matrices, refs, (layers, waves) = refs[:4], refs[4:-2], refs[-2:]
    arrived, outs = refs[: len(refs) // 2], refs[len(refs) // 2 :]
    window = incident.shape[1]
    ahead = [matrices[0][...], matrices[1][...]]
    back = [matrices[2][...], matrices[3][...]]
    depth = lax.axis_index("depth")

    def transform(value, exact):
        return from_right(*from_left(*value, ahead, exact), back, exact)

    def inverse(value, exact):
        return from_right(*from_left(*value, back, exact), ahead, exact)

    half, _ = edge_half(placed(codes, depths - 1)[0], strip)
    half = pl.multiple_of(half, BAND)
    other = pl.multiple_of(window - BAND - half, BAND)
    whole = pl.ds(0, window)

    def shares(values):
        count = len(values) - depths
        for place, value in enumerate(values):
            split_place = place < 2 * count
            mask = order[place % count] if split_place else order[place - count]
            rows = whole if not split_place else pl.ds(half if place < count else other, BAND)
            yield value, depth ^ mask, rows

    for value, index, rows in shares(arrived):
        layers[index, :, rows] = value[...].astype(jnp.float32)
    real, imag = incident[0], incident[1]
    cosine, sine = turn[0], turn[1]
    scale = 1.0 / window
    for index in range(depths):
        waves[index, 0], waves[index, 1] = real, imag
        layer_real, layer_imag = layers[index, 0], layers[index, 1]
        mixed = (real * layer_real - imag * layer_imag, real * layer_imag + imag * layer_real)
        real, imag = transform(mixed, True)
        if index + 1 < depths:
            turned = (real * cosine - imag * sine, imag * cosine + real * sine)
            real, imag = inverse(turned, True)
    real, imag = real * scale, imag * scale
    misfit = (real * real + imag * imag - measured[depth]) * scale
    adjoint = inverse((misfit * real, misfit * imag), False)
    for index in reversed(range(depths)):
        adj_real, adj_imag = adjoint
        held_real, held_imag = waves[index, 0], waves[index, 1]
        waves[index, 0] = held_real * adj_real + held_imag * adj_imag
        waves[index, 1] = held_real * adj_imag - held_imag * adj_real
        if index > 0:
            layer_real, layer_imag = layers[index, 0], layers[index, 1]
            real, imag = transform(
                (layer_real * adj_real + layer_imag * adj_imag, layer_real * adj_imag - layer_imag * adj_real),
                False,
            )
            adjoint = inverse((real * cosine + imag * sine, imag * cosine - real * sine), False)
    for value, index, rows in shares(outs):
        value[...] = waves[index, :, rows].astype(jnp.bfloat16)


def added(wide, part, block, rows, value, offset, lane):
    value = pltpu.roll(value, offset, 1)
    wide[part, block, rows] += jnp.where(lane >= offset, value, 0.0)
    wide[part, block + 1, rows] += jnp.where(lane < offset, value, 0.0)


def shed_kernel(strip, codes, *refs):
    arrived, (outer, inner, wide) = refs[:-3], refs[-3:]
    columns = outer.shape[3]
    odd = lax.rem(lax.axis_index("tile"), 2)
    wide[:, :, :BAND] = jnp.zeros_like(wide[:, :, :BAND])
    wide[:, :, BAND + strip :] = jnp.zeros_like(wide[:, :, :BAND])
    lane = lax.broadcasted_iota(jnp.int32, (BAND, LANES), 1)
    for place, value in enumerate(arrived):
        row, block, offset = placed(codes, place)
        half, start = edge_half(row, strip)
        half = pl.multiple_of(half, BAND)
        for part in range(2):
            piece = value[part] if value.shape[1] == BAND else value[part, pl.ds(half, BAND)]
            piece = piece.astype(jnp.float32)
            added(wide, part, block, pl.ds(start, BAND), piece, offset, lane)
    far = pl.multiple_of(odd * (strip + BAND), BAND)
    near = pl.multiple_of((1 - odd) * (strip + BAND), BAND)
    for block in range(columns // LANES):
        cols = slice(block * LANES, (block + 1) * LANES)
        for part in range(2):
            outer[part, 0, :, cols] = wide[part, block, pl.ds(far, BAND)].astype(jnp.bfloat16)
            inner[part, 0, :, cols] = wide[part, block, pl.ds(near, BAND)].astype(jnp.bfloat16)


def add_kernel(codes, *refs):
    arrived, (own, wide) = refs[:-2], refs[-2:]
    strip, columns = own.shape[2:]
    window = arrived[-1].shape[1]
    count = len(arrived) - codes.shape[0]
    wide[...] = jnp.zeros_like(wide)
    lane = lax.broadcasted_iota(jnp.int32, (window, LANES), 1)
    for place, value in enumerate(arrived):
        length = value.shape[1]
        row, block, offset = placed(codes, place % count if place < 2 * count else place - count)
        if place < 2 * count:
            half, _ = edge_half(row, strip)
            row += half if place < count else window - BAND - half
        for part in range(2):
            added(wide, part, block, pl.ds(row, length), value[part].astype(jnp.float32), offset, lane[:length])
    for block in range(columns // LANES):
        for part in range(2):
            own[part, 0, :, block * LANES : (block + 1) * LANES] = wide[part, block, BAND : BAND + strip]


def edge_kernel(own, outer, inner, out):
    strip = own.shape[2]
    odd = lax.rem(lax.axis_index("tile"), 2)
    out[...] = own[...]
    far = pl.multiple_of(odd * (strip - BAND), BAND)
    near = pl.multiple_of((1 - odd) * (strip - BAND), BAND)
    out[:, :, pl.ds(far, BAND)] += outer[...].astype(jnp.float32)
    out[:, :, pl.ds(near, BAND)] += inner[...].astype(jnp.float32)


def call(kernel, outs, operands, scratch=(), scalars=0):
    return pl.pallas_call(
        kernel,
        out_shape=outs,
        in_specs=[SMEM] * scalars + [VMEM] * (len(operands) - scalars),
        out_specs=jax.tree.map(lambda _: VMEM, outs),
        scratch_shapes=list(scratch),
        compiler_params=PARAMS,
    )(*operands)


def shards(transmission, probe_wave, fresnel_phase, measured, positions, extents):
    tiles, depths = lax.axis_size("tile"), lax.axis_size("depth")
    strip, columns = transmission.shape[2:]
    window = probe_wave.shape[1]
    assert positions.shape[0] == depths == 4 and transmission.shape[1] == 1 and tiles % 2 == 0
    assert strip == 2 * BAND == window
    order = ORDER
    wide = [pltpu.VMEM((2, columns // LANES + 1, strip + 2 * BAND, LANES), jnp.float32)]
    patch = jax.ShapeDtypeStruct((2, window, window), jnp.bfloat16)
    band = jax.ShapeDtypeStruct((2, 1, BAND, columns), jnp.bfloat16)
    odd = lax.axis_index("tile") % 2 == 1

    piece = jax.ShapeDtypeStruct((2, BAND, window), jnp.bfloat16)

    def swap(value, mask):
        if not mask:
            return value
        return lax.ppermute(value, "depth", [(d, d ^ mask) for d in range(depths)])

    def swapped(values):
        return [swap(v, mask) for v, mask in zip(values, order)]

    def outward(value):
        return lax.ppermute(value, "tile", [(t, (t - 1 + 2 * (t % 2)) % tiles) for t in range(tiles)])

    def inward(value):
        return lax.ppermute(value, "tile", [(t, t ^ 1) for t in range(tiles)])

    head, tail = transmission[:, :, :BAND], transmission[:, :, strip - BAND :]
    outer = outward(jnp.where(odd, tail, head).astype(jnp.bfloat16))
    inner = inward(jnp.where(odd, head, tail).astype(jnp.bfloat16))
    square = jax.ShapeDtypeStruct((2, window, window), jnp.float32)
    windows, codes, *early = call(
        lambda *refs: cut_kernel(order, tiles, *refs),
        [
            jax.ShapeDtypeStruct((depths, 2, window, window), jnp.float32),
            jax.ShapeDtypeStruct((depths, LANES), jnp.int32),
            *[piece] * EARLY,
        ],
        [positions.T, transmission],
        wide,
        scalars=1,
    )
    early = swapped(early)
    windows = call(
        lambda *refs: join_kernel(strip, *refs),
        [piece] * EARLY + [patch] * (depths - EARLY),
        [codes, windows, outer, inner],
        wide,
    )
    probe_wave, fresnel_phase, windows = lax.optimization_barrier((probe_wave, fresnel_phase, windows))
    incident, turn = call(
        lambda *refs: prep_kernel(strip, *refs),
        [square, square],
        [extents, codes, probe_wave, fresnel_phase],
        scalars=1,
    )
    windows = swapped(windows)
    pieces = call(
        lambda *refs: wave_kernel(order, strip, *refs),
        [piece] * (2 * LATE) + [patch] * (depths - LATE),
        [
            codes,
            incident,
            turn,
            measured,
            *map(jnp.asarray, tables(window)),
            *windows[:EARLY],
            *early,
            *windows[EARLY:],
        ],
        [pltpu.VMEM((depths, 2, window, window), jnp.float32)] * 2,
    )
    late = swapped(pieces[LATE : 2 * LATE])
    pieces = swapped([*pieces[:LATE], *pieces[2 * LATE :]])
    outer, inner = call(lambda *refs: shed_kernel(strip, *refs), [band] * 2, [codes, *pieces], wide)
    outer, inner = outward(outer), inward(inner)
    total = jax.ShapeDtypeStruct(transmission.shape, jnp.float32)
    own = call(add_kernel, total, [codes, *pieces[:LATE], *late, *pieces[LATE:]], wide)
    return call(edge_kernel, total, [own, outer, inner])


def solution(mesh):
    placed = (
        P(None, "depth", "tile", None),
        P(),
        P(),
        P("tile", None, None),
        P("tile", None),
        P("tile", None),
    )
    return jax.shard_map(
        shards,
        mesh=mesh,
        in_specs=placed,
        out_specs=P(None, "depth", "tile", None),
        check_vma=False,
    )
```

```python
import math

import jax
import jax.numpy as jnp
import numpy as np
from jax import lax
from jax.experimental import pallas as pl
from jax.experimental.pallas import tpu as pltpu
from jax.sharding import PartitionSpec as P

BAND = 64
LANES = 128
SPAN = 1 << 16
ORDER = (2, 3, 1, 0)
EARLY = 3
LATE = 2


SMEM = pl.BlockSpec(memory_space=pltpu.SMEM)
VMEM = pl.BlockSpec(memory_space=pltpu.VMEM)
HBM = pl.BlockSpec(memory_space=pltpu.HBM)
PARAMS = pltpu.CompilerParams(vmem_limit_bytes=12 << 20)


def tables(length):
    indices = np.arange(length)
    angles = (indices[:, None] * indices[None, :] % length) * (2.0 * math.pi / length)
    cosine, sine = np.cos(angles), np.sin(angles)
    ahead = np.block([[cosine, sine], [-sine, cosine]]).astype(np.float32)
    back = np.block([[cosine, -sine], [sine, cosine]]).astype(np.float32)
    found = []
    for matrix in (ahead, back):
        high = matrix.astype(jnp.bfloat16)
        found += [high, (matrix - high.astype(np.float32)).astype(jnp.bfloat16)]
    return found


def first_row(positions, probe, tile, strip, tiles):
    rows = strip * tiles
    start = positions[0, probe] - tile * strip + BAND
    start = jnp.where(start < 0, start + rows, start)
    return jnp.where(start >= rows, start - rows, start)


def placed(codes, place):
    code = codes[place : place + 1, :1][0, 0]
    row = lax.div(code, SPAN)
    column = code - row * SPAN
    block = lax.div(column, LANES)
    return row, block, column - block * LANES


def edge_half(row, strip):
    upper = row < BAND
    return jnp.where(upper, 0, BAND), jnp.where(upper, row, row + strip - BAND)


def turned_pair(wide, part, block, rows, offset, lane):
    turn = lax.rem(LANES - offset, LANES)
    left = pltpu.roll(wide[part, block, rows], turn, 1)
    right = pltpu.roll(wide[part, block + 1, rows], turn, 1)
    return jnp.where(lane < LANES - offset, left, right)


def band_kernel(order, tiles, positions_in, own, strip_out, outer, inner, codes, positions, sems):
    strip = strip_out.shape[2]
    tile, depth = lax.axis_index("tile"), lax.axis_index("depth")
    odd = lax.rem(tile, 2)
    outs, copies = (outer, inner), []
    for index, side in enumerate((odd, 1 - odd)):
        rows = pl.ds(pl.multiple_of(side * (strip - BAND), BAND), BAND)
        copies.append(pltpu.make_async_copy(own.at[:, :, rows], strip_out.at[:, :, rows], sems.at[index]))
        copies[-1].start()
    fetch = pltpu.make_async_copy(positions_in, positions, sems.at[2])
    fetch.start()
    fetch.wait()
    for place, mask in enumerate(order):
        probe = depth ^ mask
        row = first_row(positions, probe, tile, strip, tiles)
        codes[place : place + 1] = jnp.full((1, LANES), row * SPAN + positions[1, probe], jnp.int32)
    for copy, side, out in zip(copies, (odd, 1 - odd), outs):
        copy.wait()
        rows = pl.ds(pl.multiple_of(side * (strip - BAND), BAND), BAND)
        out[...] = strip_out[:, :, rows].astype(jnp.bfloat16)


def cut_kernel(codes, own, out, *refs):
    early, wide = refs[:-1], refs[-1]
    strip, columns = own.shape[2:]
    window = out.shape[2]
    for block in range(columns // LANES):
        for part in range(2):
            wide[part, block, BAND : BAND + strip] = own[part, 0, :, block * LANES : (block + 1) * LANES]
    lane = lax.broadcasted_iota(jnp.int32, (window, LANES), 1)
    for place in range(out.shape[0]):
        row, block, offset = placed(codes, place)
        for part in range(2):
            out[place, part] = turned_pair(wide, part, block, pl.ds(row, window), offset, lane)
        if place < len(early):
            half, _ = edge_half(row, strip)
            other = pl.multiple_of(window - BAND - half, BAND)
            early[place][...] = out[place, :, pl.ds(other, BAND)].astype(jnp.bfloat16)


def prep_kernel(strip, extents, codes, probe_wave, fresnel_phase, incident, turn):
    window = probe_wave.shape[1]
    row, _, _ = placed(codes, codes.shape[0] - 1)
    line = row - BAND + lax.broadcasted_iota(jnp.int32, (window, window), 0)
    inside = (line >= -extents[0, 0]) & (line < strip + extents[0, 1])
    for part in range(2):
        incident[part] = jnp.where(inside, probe_wave[part], 0.0)
    scale = 1.0 / window**2
    turn[0] = jnp.cos(fresnel_phase[...]) * scale
    turn[1] = jnp.sin(fresnel_phase[...]) * scale


def join_kernel(strip, codes, windows, outer, inner, *refs):
    outs, wide = refs[:-1], refs[-1]
    columns = outer.shape[3]
    window = windows.shape[2]
    odd = lax.rem(lax.axis_index("tile"), 2)
    for block in range(columns // LANES):
        cols = slice(block * LANES, (block + 1) * LANES)
        for part in range(2):
            far = pl.multiple_of(odd * (strip + BAND), BAND)
            near = pl.multiple_of((1 - odd) * (strip + BAND), BAND)
            wide[part, block, pl.ds(far, BAND)] = outer[part, 0, :, cols].astype(jnp.float32)
            wide[part, block, pl.ds(near, BAND)] = inner[part, 0, :, cols].astype(jnp.float32)
    lane = lax.broadcasted_iota(jnp.int32, (BAND, LANES), 1)
    line = lax.broadcasted_iota(jnp.int32, (BAND, LANES), 0)
    for place, out in enumerate(outs):
        row, block, offset = placed(codes, place)
        half, start = edge_half(row, strip)
        within = row + half + line
        outside = (within < BAND) | (within >= BAND + strip)
        half = pl.multiple_of(half, BAND)
        other = pl.multiple_of(window - BAND - half, BAND)
        for part in range(2):
            band = turned_pair(wide, part, block, pl.ds(start, BAND), offset, lane)
            joined = jnp.where(outside, band, windows[place, part, pl.ds(half, BAND)]).astype(jnp.bfloat16)
            if out.shape[1] == BAND:
                out[part] = joined
                continue
            out[part, pl.ds(half, BAND)] = joined
            out[part, pl.ds(other, BAND)] = windows[place, part, pl.ds(other, BAND)].astype(jnp.bfloat16)


def split(value):
    high = value.astype(jnp.bfloat16)
    return high, (value - high.astype(jnp.float32)).astype(jnp.bfloat16)


def dot(left, right):
    return jnp.dot(left, right, preferred_element_type=jnp.float32)


def from_left(real, imag, matrix, exact):
    half = real.shape[1]
    stacked = jnp.concatenate([real, imag], axis=0)
    if exact:
        high, low = split(stacked)
        both = dot(matrix[0], jnp.concatenate([high, low], axis=1))
        stacked = both[:, :half] + both[:, half:] + dot(matrix[1], high)
    else:
        stacked = dot(matrix[0], stacked.astype(jnp.bfloat16))
    size = real.shape[0]
    return stacked[:size], stacked[size:]


def from_right(real, imag, matrix, exact):
    size = real.shape[0]
    stacked = jnp.concatenate([real, imag], axis=1)
    if exact:
        high, low = split(stacked)
        both = dot(jnp.concatenate([high, low], axis=0), matrix[0])
        stacked = both[:size] + both[size:] + dot(high, matrix[1])
    else:
        stacked = dot(stacked.astype(jnp.bfloat16), matrix[0])
    half = real.shape[1]
    return stacked[:, :half], stacked[:, half:]


def wave_kernel(order, strip, codes, incident, turn, measured, *refs):
    depths = len(order)
    matrices, refs, (layers, waves) = refs[:4], refs[4:-2], refs[-2:]
    arrived, outs = refs[: depths + EARLY], refs[depths + EARLY :]
    window = incident.shape[1]
    ahead = [matrices[0][...], matrices[1][...]]
    back = [matrices[2][...], matrices[3][...]]
    depth = lax.axis_index("depth")

    def transform(value, exact):
        return from_right(*from_left(*value, ahead, exact), back, exact)

    def inverse(value, exact):
        return from_right(*from_left(*value, back, exact), ahead, exact)

    half, _ = edge_half(placed(codes, depths - 1)[0], strip)
    half = pl.multiple_of(half, BAND)
    other = pl.multiple_of(window - BAND - half, BAND)
    whole = pl.ds(0, window)

    def shares(values):
        count = len(values) - depths
        for place, value in enumerate(values):
            split_place = place < 2 * count
            mask = order[place % count] if split_place else order[place - count]
            rows = whole if not split_place else pl.ds(half if place < count else other, BAND)
            yield value, depth ^ mask, rows

    for value, index, rows in shares(arrived):
        layers[index, :, rows] = value[...].astype(jnp.float32)
    real, imag = incident[0], incident[1]
    cosine, sine = turn[0], turn[1]
    scale = 1.0 / window
    for index in range(depths):
        waves[index, 0], waves[index, 1] = real, imag
        layer_real, layer_imag = layers[index, 0], layers[index, 1]
        mixed = (real * layer_real - imag * layer_imag, real * layer_imag + imag * layer_real)
        real, imag = transform(mixed, True)
        if index + 1 < depths:
            turned = (real * cosine - imag * sine, imag * cosine + real * sine)
            real, imag = inverse(turned, True)
    real, imag = real * scale, imag * scale
    misfit = (real * real + imag * imag - measured[depth]) * scale
    adjoint = inverse((misfit * real, misfit * imag), False)
    for index in reversed(range(depths)):
        adj_real, adj_imag = adjoint
        held_real, held_imag = waves[index, 0], waves[index, 1]
        waves[index, 0] = held_real * adj_real + held_imag * adj_imag
        waves[index, 1] = held_real * adj_imag - held_imag * adj_real
        if index > 0:
            layer_real, layer_imag = layers[index, 0], layers[index, 1]
            real, imag = transform(
                (layer_real * adj_real + layer_imag * adj_imag, layer_real * adj_imag - layer_imag * adj_real),
                False,
            )
            adjoint = inverse((real * cosine + imag * sine, imag * cosine - real * sine), False)
    for value, index, rows in shares(outs):
        value[...] = waves[index, :, rows].astype(jnp.bfloat16)


def added(wide, part, block, rows, value, offset, lane):
    value = pltpu.roll(value, offset, 1)
    wide[part, block, rows] += jnp.where(lane >= offset, value, 0.0)
    wide[part, block + 1, rows] += jnp.where(lane < offset, value, 0.0)


def shed_kernel(strip, codes, *refs):
    arrived, (outer, inner, wide) = refs[:-3], refs[-3:]
    columns = outer.shape[3]
    odd = lax.rem(lax.axis_index("tile"), 2)
    wide[:, :, :BAND] = jnp.zeros_like(wide[:, :, :BAND])
    wide[:, :, BAND + strip :] = jnp.zeros_like(wide[:, :, :BAND])
    lane = lax.broadcasted_iota(jnp.int32, (BAND, LANES), 1)
    for place, value in enumerate(arrived):
        row, block, offset = placed(codes, place)
        half, start = edge_half(row, strip)
        half = pl.multiple_of(half, BAND)
        for part in range(2):
            piece = value[part] if value.shape[1] == BAND else value[part, pl.ds(half, BAND)]
            piece = piece.astype(jnp.float32)
            added(wide, part, block, pl.ds(start, BAND), piece, offset, lane)
    far = pl.multiple_of(odd * (strip + BAND), BAND)
    near = pl.multiple_of((1 - odd) * (strip + BAND), BAND)
    for block in range(columns // LANES):
        cols = slice(block * LANES, (block + 1) * LANES)
        for part in range(2):
            outer[part, 0, :, cols] = wide[part, block, pl.ds(far, BAND)].astype(jnp.bfloat16)
            inner[part, 0, :, cols] = wide[part, block, pl.ds(near, BAND)].astype(jnp.bfloat16)


def add_kernel(codes, *refs):
    arrived, (own, wide) = refs[:-2], refs[-2:]
    strip, columns = own.shape[2:]
    window = arrived[-1].shape[1]
    count = len(arrived) - codes.shape[0]
    wide[...] = jnp.zeros_like(wide)
    lane = lax.broadcasted_iota(jnp.int32, (window, LANES), 1)
    for place, value in enumerate(arrived):
        length = value.shape[1]
        row, block, offset = placed(codes, place % count if place < 2 * count else place - count)
        if place < 2 * count:
            half, _ = edge_half(row, strip)
            row += half if place < count else window - BAND - half
        for part in range(2):
            added(wide, part, block, pl.ds(row, length), value[part].astype(jnp.float32), offset, lane[:length])
    for block in range(columns // LANES):
        for part in range(2):
            own[part, 0, :, block * LANES : (block + 1) * LANES] = wide[part, block, BAND : BAND + strip]


def edge_kernel(side, own, band, *refs):
    out, summed, sem = refs[-3:]
    odd = lax.rem(lax.axis_index("tile"), 2)
    rows = pl.ds(pl.multiple_of((odd if side == 0 else 1 - odd) * (own.shape[2] - BAND), BAND), BAND)
    summed[...] = own[:, :, rows] + band[...].astype(jnp.float32)
    copy = pltpu.make_async_copy(summed, out.at[:, :, rows], sem)
    copy.start()
    copy.wait()


def edge(side, own, band, *partial):
    return pl.pallas_call(
        lambda *refs: edge_kernel(side, *refs),
        out_shape=jax.ShapeDtypeStruct(own.shape, own.dtype),
        in_specs=[VMEM, VMEM] + [HBM] * len(partial),
        out_specs=HBM,
        scratch_shapes=[pltpu.VMEM(band.shape, own.dtype), pltpu.SemaphoreType.DMA],
        input_output_aliases={2: 0} if partial else {},
        compiler_params=PARAMS,
    )(own, band, *partial)


def call(kernel, outs, operands, scratch=(), scalars=0):
    return pl.pallas_call(
        kernel,
        out_shape=outs,
        in_specs=[SMEM] * scalars + [VMEM] * (len(operands) - scalars),
        out_specs=jax.tree.map(lambda _: VMEM, outs),
        scratch_shapes=list(scratch),
        compiler_params=PARAMS,
    )(*operands)


def shards(transmission, probe_wave, fresnel_phase, measured, positions, extents):
    tiles, depths = lax.axis_size("tile"), lax.axis_size("depth")
    strip, columns = transmission.shape[2:]
    window = probe_wave.shape[1]
    assert positions.shape[0] == depths == 4 and transmission.shape[1] == 1 and tiles % 2 == 0
    assert strip == 2 * BAND == window
    order = ORDER
    wide = [pltpu.VMEM((2, columns // LANES + 1, strip + 2 * BAND, LANES), jnp.float32)]
    patch = jax.ShapeDtypeStruct((2, window, window), jnp.bfloat16)
    band = jax.ShapeDtypeStruct((2, 1, BAND, columns), jnp.bfloat16)

    piece = jax.ShapeDtypeStruct((2, BAND, window), jnp.bfloat16)

    def swap(value, mask):
        if not mask:
            return value
        return lax.ppermute(value, "depth", [(d, d ^ mask) for d in range(depths)])

    def swapped(values):
        return [swap(v, mask) for v, mask in zip(values, order)]

    def outward(value):
        return lax.ppermute(value, "tile", [(t, (t - 1 + 2 * (t % 2)) % tiles) for t in range(tiles)])

    def inward(value):
        return lax.ppermute(value, "tile", [(t, t ^ 1) for t in range(tiles)])

    places = jax.ShapeDtypeStruct((depths, LANES), jnp.int32)
    total = jax.ShapeDtypeStruct(transmission.shape, jnp.float32)
    own, outer, inner, codes = pl.pallas_call(
        lambda *refs: band_kernel(order, tiles, *refs),
        out_shape=[total, band, band, places],
        in_specs=[HBM, HBM],
        out_specs=[VMEM] * 4,
        scratch_shapes=[pltpu.SMEM((2, depths), jnp.int32), pltpu.SemaphoreType.DMA((3,))],
        compiler_params=PARAMS,
        name="bands",
    )(*(pltpu.with_memory_space_constraint(v, pltpu.HBM) for v in (positions.T, transmission)))
    outer, inner = outward(outer), inward(inner)
    square = jax.ShapeDtypeStruct((2, window, window), jnp.float32)
    full = jax.ShapeDtypeStruct((depths, 2, window, window), jnp.float32)
    windows, *early = call(cut_kernel, [full] + [piece] * EARLY, [codes, own], wide)
    early = swapped(early)
    windows = call(
        lambda *refs: join_kernel(strip, *refs),
        [piece] * EARLY + [patch] * (depths - EARLY),
        [codes, windows, outer, inner],
        wide,
    )
    probe_wave, fresnel_phase, windows = lax.optimization_barrier((probe_wave, fresnel_phase, windows))
    incident, turn = call(
        lambda *refs: prep_kernel(strip, *refs),
        [square, square],
        [extents, codes, probe_wave, fresnel_phase],
        scalars=1,
    )
    windows = swapped(windows)
    pieces = call(
        lambda *refs: wave_kernel(order, strip, *refs),
        [piece] * (2 * LATE) + [patch] * (depths - LATE),
        [
            codes,
            incident,
            turn,
            measured,
            *map(jnp.asarray, tables(window)),
            *windows[:EARLY],
            *early,
            *windows[EARLY:],
        ],
        [pltpu.VMEM((depths, 2, window, window), jnp.float32)] * 2,
    )
    late = swapped(pieces[LATE : 2 * LATE])
    pieces = swapped([*pieces[:LATE], *pieces[2 * LATE :]])
    outer, inner = call(lambda *refs: shed_kernel(strip, *refs), [band] * 2, [codes, *pieces], wide)
    outer, inner = outward(outer), inward(inner)
    own = call(add_kernel, total, [codes, *pieces[:LATE], *late, *pieces[LATE:]], wide)
    return edge(0, own, outer, edge(1, own, inner))


def solution(mesh):
    placed = (
        P(None, "depth", "tile", None),
        P(),
        P(),
        P("tile", None, None),
        P("tile", None),
        P("tile", None),
    )
    return jax.shard_map(
        shards,
        mesh=mesh,
        in_specs=placed,
        out_specs=P(None, "depth", "tile", None),
        check_vma=False,
    )
```

```python
import math

import jax
import jax.numpy as jnp
import numpy as np
from jax import lax
from jax.experimental import pallas as pl
from jax.experimental.pallas import tpu as pltpu
from jax.sharding import PartitionSpec as P

BAND = 64
LANES = 128
SPAN = 1 << 16
ORDER = (2, 3, 1, 0)
EARLY = 3
LATE = 2


SMEM = pl.BlockSpec(memory_space=pltpu.SMEM)
VMEM = pl.BlockSpec(memory_space=pltpu.VMEM)
HBM = pl.BlockSpec(memory_space=pltpu.HBM)
PARAMS = pltpu.CompilerParams(vmem_limit_bytes=12 << 20)


def tables(length):
    indices = np.arange(length)
    angles = (indices[:, None] * indices[None, :] % length) * (2.0 * math.pi / length)
    cosine, sine = np.cos(angles), np.sin(angles)
    ahead = np.block([[cosine, sine], [-sine, cosine]]).astype(np.float32)
    back = np.block([[cosine, -sine], [sine, cosine]]).astype(np.float32)
    found = []
    for matrix in (ahead, back):
        high = matrix.astype(jnp.bfloat16)
        found += [high, (matrix - high.astype(np.float32)).astype(jnp.bfloat16)]
    return found


def first_row(positions, probe, tile, strip, tiles):
    rows = strip * tiles
    start = positions[0, probe] - tile * strip + BAND
    start = jnp.where(start < 0, start + rows, start)
    return jnp.where(start >= rows, start - rows, start)


def placed(codes, place):
    code = codes[place : place + 1, :1][0, 0]
    row = lax.div(code, SPAN)
    column = code - row * SPAN
    block = lax.div(column, LANES)
    return row, block, column - block * LANES


def edge_half(row, strip):
    upper = row < BAND
    return jnp.where(upper, 0, BAND), jnp.where(upper, row, row + strip - BAND)


def turned_pair(wide, part, block, rows, offset, lane):
    turn = lax.rem(LANES - offset, LANES)
    left = pltpu.roll(wide[part, block, rows], turn, 1)
    right = pltpu.roll(wide[part, block + 1, rows], turn, 1)
    return jnp.where(lane < LANES - offset, left, right)


def band_kernel(order, tiles, positions_in, own, strip_out, outer, inner, codes, positions, sems):
    strip = strip_out.shape[2]
    tile, depth = lax.axis_index("tile"), lax.axis_index("depth")
    odd = lax.rem(tile, 2)
    outs, copies = (outer, inner), []
    for index, side in enumerate((odd, 1 - odd)):
        rows = pl.ds(pl.multiple_of(side * (strip - BAND), BAND), BAND)
        copies.append(pltpu.make_async_copy(own.at[:, :, rows], strip_out.at[:, :, rows], sems.at[index]))
        copies[-1].start()
    fetch = pltpu.make_async_copy(positions_in, positions, sems.at[2])
    fetch.start()
    fetch.wait()
    for place, mask in enumerate(order):
        probe = depth ^ mask
        row = first_row(positions, probe, tile, strip, tiles)
        codes[place : place + 1] = jnp.full((1, LANES), row * SPAN + positions[1, probe], jnp.int32)
    for copy, side, out in zip(copies, (odd, 1 - odd), outs):
        copy.wait()
        rows = pl.ds(pl.multiple_of(side * (strip - BAND), BAND), BAND)
        out[...] = strip_out[:, :, rows].astype(jnp.bfloat16)


def cut_kernel(codes, own, out, *refs):
    early, wide = refs[:-1], refs[-1]
    strip, columns = own.shape[2:]
    window = out.shape[2]
    for block in range(columns // LANES):
        for part in range(2):
            wide[part, block, BAND : BAND + strip] = own[part, 0, :, block * LANES : (block + 1) * LANES]
    lane = lax.broadcasted_iota(jnp.int32, (window, LANES), 1)
    for place in range(out.shape[0]):
        row, block, offset = placed(codes, place)
        for part in range(2):
            out[place, part] = turned_pair(wide, part, block, pl.ds(row, window), offset, lane)
        if place < len(early):
            half, _ = edge_half(row, strip)
            other = pl.multiple_of(window - BAND - half, BAND)
            early[place][...] = out[place, :, pl.ds(other, BAND)].astype(jnp.bfloat16)


def prep_kernel(strip, extents, codes, probe_wave, fresnel_phase, incident, turn, upper):
    window = probe_wave.shape[1]
    row, _, _ = placed(codes, codes.shape[0] - 1)
    line = row - BAND + lax.broadcasted_iota(jnp.int32, (window, window), 0)
    inside = (line >= -extents[0, 0]) & (line < strip + extents[0, 1])
    for part in range(2):
        incident[part] = jnp.where(inside, probe_wave[part], 0.0)
    upper[...] = jnp.full(upper.shape, row < BAND).astype(jnp.float32)
    scale = 1.0 / window**2
    turn[0] = jnp.cos(fresnel_phase[...]) * scale
    turn[1] = jnp.sin(fresnel_phase[...]) * scale


def join_kernel(strip, codes, windows, outer, inner, *refs):
    outs, wide = refs[:-1], refs[-1]
    columns = outer.shape[3]
    window = windows.shape[2]
    odd = lax.rem(lax.axis_index("tile"), 2)
    for block in range(columns // LANES):
        cols = slice(block * LANES, (block + 1) * LANES)
        for part in range(2):
            far = pl.multiple_of(odd * (strip + BAND), BAND)
            near = pl.multiple_of((1 - odd) * (strip + BAND), BAND)
            wide[part, block, pl.ds(far, BAND)] = outer[part, 0, :, cols].astype(jnp.float32)
            wide[part, block, pl.ds(near, BAND)] = inner[part, 0, :, cols].astype(jnp.float32)
    lane = lax.broadcasted_iota(jnp.int32, (BAND, LANES), 1)
    line = lax.broadcasted_iota(jnp.int32, (BAND, LANES), 0)
    for place, out in enumerate(outs):
        row, block, offset = placed(codes, place)
        half, start = edge_half(row, strip)
        within = row + half + line
        outside = (within < BAND) | (within >= BAND + strip)
        half = pl.multiple_of(half, BAND)
        other = pl.multiple_of(window - BAND - half, BAND)
        for part in range(2):
            band = turned_pair(wide, part, block, pl.ds(start, BAND), offset, lane)
            joined = jnp.where(outside, band, windows[place, part, pl.ds(half, BAND)]).astype(jnp.bfloat16)
            if out.shape[1] == BAND:
                out[part] = joined
                continue
            out[part, pl.ds(half, BAND)] = joined
            out[part, pl.ds(other, BAND)] = windows[place, part, pl.ds(other, BAND)].astype(jnp.bfloat16)


def split(value):
    high = value.astype(jnp.bfloat16)
    return high, (value - high.astype(jnp.float32)).astype(jnp.bfloat16)


def dot(left, right):
    return jnp.dot(left, right, preferred_element_type=jnp.float32)


def from_left(real, imag, matrix, exact):
    half = real.shape[1]
    stacked = jnp.concatenate([real, imag], axis=0)
    if exact:
        high, low = split(stacked)
        both = dot(matrix[0], jnp.concatenate([high, low], axis=1))
        stacked = both[:, :half] + both[:, half:] + dot(matrix[1], high)
    else:
        stacked = dot(matrix[0], stacked.astype(jnp.bfloat16))
    size = real.shape[0]
    return stacked[:size], stacked[size:]


def from_right(real, imag, matrix, exact):
    stacked = jnp.concatenate([real, imag], axis=1).astype(jnp.bfloat16)
    product = dot(stacked, matrix[0])
    if exact:
        product += dot(stacked, matrix[1])
    half = real.shape[1]
    return product[:, :half], product[:, half:]


def wave_kernel(order, incident, turn, upper, measured, *refs):
    depths = len(order)
    matrices, refs, (layers, waves) = refs[:4], refs[4:-2], refs[-2:]
    arrived, outs = refs[: depths + EARLY], refs[depths + EARLY :]
    window = incident.shape[1]
    ahead = [matrices[0][...], matrices[1][...]]
    back = [matrices[2][...], matrices[3][...]]
    depth = lax.axis_index("depth")

    def transform(value, exact):
        return from_right(*from_left(*value, ahead, exact), back, exact)

    def inverse(value, exact):
        return from_right(*from_left(*value, back, exact), ahead, exact)

    above = upper[...] != 0.0
    for place, mask in enumerate(order):
        index = depth ^ mask
        if place < EARLY:
            edge_rows, own_rows = (arrived[p][...].astype(jnp.float32) for p in (place, EARLY + place))
            layers[index, :, :BAND] = jnp.where(above, edge_rows, own_rows)
            layers[index, :, BAND:] = jnp.where(above, own_rows, edge_rows)
        else:
            layers[index] = arrived[EARLY + place][...].astype(jnp.float32)
    real, imag = incident[0], incident[1]
    cosine, sine = turn[0], turn[1]
    scale = 1.0 / window
    for index in range(depths):
        waves[index, 0], waves[index, 1] = real, imag
        layer_real, layer_imag = layers[index, 0], layers[index, 1]
        mixed = (real * layer_real - imag * layer_imag, real * layer_imag + imag * layer_real)
        real, imag = transform(mixed, True)
        if index + 1 < depths:
            turned = (real * cosine - imag * sine, imag * cosine + real * sine)
            real, imag = inverse(turned, True)
    real, imag = real * scale, imag * scale
    misfit = (real * real + imag * imag - measured[depth]) * scale
    adjoint = inverse((misfit * real, misfit * imag), False)
    for index in reversed(range(depths)):
        adj_real, adj_imag = adjoint
        held_real, held_imag = waves[index, 0], waves[index, 1]
        waves[index, 0] = held_real * adj_real + held_imag * adj_imag
        waves[index, 1] = held_real * adj_imag - held_imag * adj_real
        if index > 0:
            layer_real, layer_imag = layers[index, 0], layers[index, 1]
            real, imag = transform(
                (layer_real * adj_real + layer_imag * adj_imag, layer_real * adj_imag - layer_imag * adj_real),
                False,
            )
            adjoint = inverse((real * cosine + imag * sine, imag * cosine - real * sine), False)
    for place, mask in enumerate(order):
        index = depth ^ mask
        if place < LATE:
            first, second = waves[index, :, :BAND], waves[index, :, BAND:]
            outs[place][...] = jnp.where(above, first, second).astype(jnp.bfloat16)
            outs[LATE + place][...] = jnp.where(above, second, first).astype(jnp.bfloat16)
        else:
            outs[LATE + place][...] = waves[index].astype(jnp.bfloat16)


def added(wide, part, block, rows, value, offset, lane):
    value = pltpu.roll(value, offset, 1)
    wide[part, block, rows] += jnp.where(lane >= offset, value, 0.0)
    wide[part, block + 1, rows] += jnp.where(lane < offset, value, 0.0)


def shed_kernel(strip, codes, *refs):
    arrived, (outer, inner, wide) = refs[:-3], refs[-3:]
    columns = outer.shape[3]
    odd = lax.rem(lax.axis_index("tile"), 2)
    wide[:, :, :BAND] = jnp.zeros_like(wide[:, :, :BAND])
    wide[:, :, BAND + strip :] = jnp.zeros_like(wide[:, :, :BAND])
    lane = lax.broadcasted_iota(jnp.int32, (BAND, LANES), 1)
    for place, value in enumerate(arrived):
        row, block, offset = placed(codes, place)
        half, start = edge_half(row, strip)
        half = pl.multiple_of(half, BAND)
        for part in range(2):
            piece = value[part] if value.shape[1] == BAND else value[part, pl.ds(half, BAND)]
            piece = piece.astype(jnp.float32)
            added(wide, part, block, pl.ds(start, BAND), piece, offset, lane)
    far = pl.multiple_of(odd * (strip + BAND), BAND)
    near = pl.multiple_of((1 - odd) * (strip + BAND), BAND)
    for block in range(columns // LANES):
        cols = slice(block * LANES, (block + 1) * LANES)
        for part in range(2):
            outer[part, 0, :, cols] = wide[part, block, pl.ds(far, BAND)].astype(jnp.bfloat16)
            inner[part, 0, :, cols] = wide[part, block, pl.ds(near, BAND)].astype(jnp.bfloat16)


def add_kernel(codes, *refs):
    arrived, (own, wide) = refs[:-2], refs[-2:]
    strip, columns = own.shape[2:]
    window = arrived[-1].shape[1]
    count = len(arrived) - codes.shape[0]
    wide[...] = jnp.zeros_like(wide)
    lane = lax.broadcasted_iota(jnp.int32, (window, LANES), 1)
    for place, value in enumerate(arrived):
        length = value.shape[1]
        row, block, offset = placed(codes, place % count if place < 2 * count else place - count)
        if place < 2 * count:
            half, _ = edge_half(row, strip)
            row += half if place < count else window - BAND - half
        for part in range(2):
            added(wide, part, block, pl.ds(row, length), value[part].astype(jnp.float32), offset, lane[:length])
    for block in range(columns // LANES):
        for part in range(2):
            own[part, 0, :, block * LANES : (block + 1) * LANES] = wide[part, block, BAND : BAND + strip]


def edge_kernel(side, own, band, *refs):
    out, summed, sem = refs[-3:]
    odd = lax.rem(lax.axis_index("tile"), 2)
    rows = pl.ds(pl.multiple_of((odd if side == 0 else 1 - odd) * (own.shape[2] - BAND), BAND), BAND)
    summed[...] = own[:, :, rows] + band[...].astype(jnp.float32)
    copy = pltpu.make_async_copy(summed, out.at[:, :, rows], sem)
    copy.start()
    copy.wait()


def edge(side, own, band, *partial):
    return pl.pallas_call(
        lambda *refs: edge_kernel(side, *refs),
        out_shape=jax.ShapeDtypeStruct(own.shape, own.dtype),
        in_specs=[VMEM, VMEM] + [HBM] * len(partial),
        out_specs=HBM,
        scratch_shapes=[pltpu.VMEM(band.shape, own.dtype), pltpu.SemaphoreType.DMA],
        input_output_aliases={2: 0} if partial else {},
        compiler_params=PARAMS,
    )(own, band, *partial)


def call(kernel, outs, operands, scratch=(), scalars=0):
    return pl.pallas_call(
        kernel,
        out_shape=outs,
        in_specs=[SMEM] * scalars + [VMEM] * (len(operands) - scalars),
        out_specs=jax.tree.map(lambda _: VMEM, outs),
        scratch_shapes=list(scratch),
        compiler_params=PARAMS,
    )(*operands)


def shards(transmission, probe_wave, fresnel_phase, measured, positions, extents):
    tiles, depths = lax.axis_size("tile"), lax.axis_size("depth")
    strip, columns = transmission.shape[2:]
    window = probe_wave.shape[1]
    assert positions.shape[0] == depths == 4 and transmission.shape[1] == 1 and tiles % 2 == 0
    assert strip == 2 * BAND == window
    order = ORDER
    wide = [pltpu.VMEM((2, columns // LANES + 1, strip + 2 * BAND, LANES), jnp.float32)]
    patch = jax.ShapeDtypeStruct((2, window, window), jnp.bfloat16)
    band = jax.ShapeDtypeStruct((2, 1, BAND, columns), jnp.bfloat16)

    piece = jax.ShapeDtypeStruct((2, BAND, window), jnp.bfloat16)

    def swap(value, mask):
        if not mask:
            return value
        return lax.ppermute(value, "depth", [(d, d ^ mask) for d in range(depths)])

    def swapped(values):
        return [swap(v, mask) for v, mask in zip(values, order)]

    def outward(value):
        return lax.ppermute(value, "tile", [(t, (t - 1 + 2 * (t % 2)) % tiles) for t in range(tiles)])

    def inward(value):
        return lax.ppermute(value, "tile", [(t, t ^ 1) for t in range(tiles)])

    places = jax.ShapeDtypeStruct((depths, LANES), jnp.int32)
    total = jax.ShapeDtypeStruct(transmission.shape, jnp.float32)
    own, outer, inner, codes = pl.pallas_call(
        lambda *refs: band_kernel(order, tiles, *refs),
        out_shape=[total, band, band, places],
        in_specs=[HBM, HBM],
        out_specs=[VMEM] * 4,
        scratch_shapes=[pltpu.SMEM((2, depths), jnp.int32), pltpu.SemaphoreType.DMA((3,))],
        compiler_params=PARAMS,
        name="bands",
    )(*(pltpu.with_memory_space_constraint(v, pltpu.HBM) for v in (positions.T, transmission)))
    outer, inner = outward(outer), inward(inner)
    square = jax.ShapeDtypeStruct((2, window, window), jnp.float32)
    full = jax.ShapeDtypeStruct((depths, 2, window, window), jnp.float32)
    windows, *early = call(cut_kernel, [full] + [piece] * EARLY, [codes, own], wide)
    early = swapped(early)
    windows = call(
        lambda *refs: join_kernel(strip, *refs),
        [piece] * EARLY + [patch] * (depths - EARLY),
        [codes, windows, outer, inner],
        wide,
    )
    probe_wave, fresnel_phase, windows = lax.optimization_barrier((probe_wave, fresnel_phase, windows))
    incident, turn, upper = call(
        lambda *refs: prep_kernel(strip, *refs),
        [square, square, jax.ShapeDtypeStruct((BAND, window), jnp.float32)],
        [extents, codes, probe_wave, fresnel_phase],
        scalars=1,
    )
    windows = swapped(windows)
    pieces = call(
        lambda *refs: wave_kernel(order, *refs),
        [piece] * (2 * LATE) + [patch] * (depths - LATE),
        [
            incident,
            turn,
            upper,
            measured,
            *map(jnp.asarray, tables(window)),
            *windows[:EARLY],
            *early,
            *windows[EARLY:],
        ],
        [pltpu.VMEM((depths, 2, window, window), jnp.float32)] * 2,
    )
    late = swapped(pieces[LATE : 2 * LATE])
    pieces = swapped([*pieces[:LATE], *pieces[2 * LATE :]])
    outer, inner = call(lambda *refs: shed_kernel(strip, *refs), [band] * 2, [codes, *pieces], wide)
    outer, inner = outward(outer), inward(inner)
    own = call(add_kernel, total, [codes, *pieces[:LATE], *late, *pieces[LATE:]], wide)
    return edge(0, own, outer, edge(1, own, inner))


def solution(mesh):
    placed = (
        P(None, "depth", "tile", None),
        P(),
        P(),
        P("tile", None, None),
        P("tile", None),
        P("tile", None),
    )
    return jax.shard_map(
        shards,
        mesh=mesh,
        in_specs=placed,
        out_specs=P(None, "depth", "tile", None),
        check_vma=False,
    )
```

```python
import math

import jax
import jax.numpy as jnp
import numpy as np
from jax import lax
from jax.experimental import pallas as pl
from jax.experimental.pallas import tpu as pltpu
from jax.sharding import PartitionSpec as P

BAND = 64
LANES = 128
SPAN = 1 << 16
ORDER = (2, 3, 1, 0)
EARLY = 3
LATE = 2


SMEM = pl.BlockSpec(memory_space=pltpu.SMEM)
VMEM = pl.BlockSpec(memory_space=pltpu.VMEM)
HBM = pl.BlockSpec(memory_space=pltpu.HBM)
PARAMS = pltpu.CompilerParams(vmem_limit_bytes=12 << 20)


def tables(length):
    indices = np.arange(length)
    angles = (indices[:, None] * indices[None, :] % length) * (2.0 * math.pi / length)
    cosine, sine = np.cos(angles), np.sin(angles)
    ahead = np.block([[cosine, sine], [-sine, cosine]]).astype(np.float32)
    back = np.block([[cosine, -sine], [sine, cosine]]).astype(np.float32)
    found = []
    for matrix in (ahead, back):
        high = matrix.astype(jnp.bfloat16)
        found += [high, (matrix - high.astype(np.float32)).astype(jnp.bfloat16)]
    return found


def first_row(positions, probe, tile, strip, tiles):
    rows = strip * tiles
    start = positions[0, probe] - tile * strip + BAND
    start = jnp.where(start < 0, start + rows, start)
    return jnp.where(start >= rows, start - rows, start)


def placed(codes, place):
    code = codes[place : place + 1, :1][0, 0]
    row = lax.div(code, SPAN)
    column = code - row * SPAN
    block = lax.div(column, LANES)
    return row, block, column - block * LANES


def edge_half(row, strip):
    upper = row < BAND
    return jnp.where(upper, 0, BAND), jnp.where(upper, row, row + strip - BAND)


def turned_pair(wide, part, block, rows, offset, lane):
    turn = lax.rem(LANES - offset, LANES)
    left = pltpu.roll(wide[part, block, rows], turn, 1)
    right = pltpu.roll(wide[part, block + 1, rows], turn, 1)
    return jnp.where(lane < LANES - offset, left, right)


def band_kernel(order, tiles, positions_in, own, strip_out, outer, inner, codes, positions, sems):
    strip = strip_out.shape[2]
    tile, depth = lax.axis_index("tile"), lax.axis_index("depth")
    odd = lax.rem(tile, 2)
    outs, copies = (outer, inner), []
    fetch = pltpu.make_async_copy(positions_in, positions, sems.at[2])
    fetch.start()
    for index, side in enumerate((odd, 1 - odd)):
        rows = pl.ds(pl.multiple_of(side * (strip - BAND), BAND), BAND)
        copies.append(pltpu.make_async_copy(own.at[:, :, rows], strip_out.at[:, :, rows], sems.at[index]))
        copies[-1].start()
    fetch.wait()
    for place, mask in enumerate(order):
        probe = depth ^ mask
        row = first_row(positions, probe, tile, strip, tiles)
        codes[place : place + 1] = jnp.full((1, LANES), row * SPAN + positions[1, probe], jnp.int32)
    for copy, side, out in zip(copies, (odd, 1 - odd), outs):
        copy.wait()
        rows = pl.ds(pl.multiple_of(side * (strip - BAND), BAND), BAND)
        out[...] = strip_out[:, :, rows].astype(jnp.bfloat16)


def cut_kernel(codes, own, out, *refs):
    early, wide = refs[:-1], refs[-1]
    strip, columns = own.shape[2:]
    window = out.shape[2]
    for block in range(columns // LANES):
        for part in range(2):
            wide[part, block, BAND : BAND + strip] = own[part, 0, :, block * LANES : (block + 1) * LANES]
    lane = lax.broadcasted_iota(jnp.int32, (window, LANES), 1)
    for place in range(out.shape[0]):
        row, block, offset = placed(codes, place)
        for part in range(2):
            out[place, part] = turned_pair(wide, part, block, pl.ds(row, window), offset, lane)
        if place < len(early):
            half, _ = edge_half(row, strip)
            other = pl.multiple_of(window - BAND - half, BAND)
            early[place][...] = out[place, :, pl.ds(other, BAND)].astype(jnp.bfloat16)


def prep_kernel(strip, extents, codes, probe_wave, fresnel_phase, incident, turn, upper):
    window = probe_wave.shape[1]
    row, _, _ = placed(codes, codes.shape[0] - 1)
    line = row - BAND + lax.broadcasted_iota(jnp.int32, (window, window), 0)
    inside = (line >= -extents[0, 0]) & (line < strip + extents[0, 1])
    for part in range(2):
        incident[part] = jnp.where(inside, probe_wave[part], 0.0)
    upper[...] = jnp.full(upper.shape, row < BAND).astype(jnp.float32)
    scale = 1.0 / window**2
    turn[0] = jnp.cos(fresnel_phase[...]) * scale
    turn[1] = jnp.sin(fresnel_phase[...]) * scale


def join_kernel(strip, codes, windows, outer, inner, *refs):
    outs, wide = refs[:-1], refs[-1]
    columns = outer.shape[3]
    window = windows.shape[2]
    odd = lax.rem(lax.axis_index("tile"), 2)
    for block in range(columns // LANES):
        cols = slice(block * LANES, (block + 1) * LANES)
        for part in range(2):
            far = pl.multiple_of(odd * (strip + BAND), BAND)
            near = pl.multiple_of((1 - odd) * (strip + BAND), BAND)
            wide[part, block, pl.ds(far, BAND)] = outer[part, 0, :, cols].astype(jnp.float32)
            wide[part, block, pl.ds(near, BAND)] = inner[part, 0, :, cols].astype(jnp.float32)
    lane = lax.broadcasted_iota(jnp.int32, (BAND, LANES), 1)
    line = lax.broadcasted_iota(jnp.int32, (BAND, LANES), 0)
    for place, out in enumerate(outs):
        row, block, offset = placed(codes, place)
        half, start = edge_half(row, strip)
        within = row + half + line
        outside = (within < BAND) | (within >= BAND + strip)
        half = pl.multiple_of(half, BAND)
        other = pl.multiple_of(window - BAND - half, BAND)
        for part in range(2):
            band = turned_pair(wide, part, block, pl.ds(start, BAND), offset, lane)
            joined = jnp.where(outside, band, windows[place, part, pl.ds(half, BAND)]).astype(jnp.bfloat16)
            if out.shape[1] == BAND:
                out[part] = joined
                continue
            out[part, pl.ds(half, BAND)] = joined
            out[part, pl.ds(other, BAND)] = windows[place, part, pl.ds(other, BAND)].astype(jnp.bfloat16)


def split(value):
    high = value.astype(jnp.bfloat16)
    return high, (value - high.astype(jnp.float32)).astype(jnp.bfloat16)


def dot(left, right):
    return jnp.dot(left, right, preferred_element_type=jnp.float32)


def from_left(real, imag, matrix, exact):
    size = real.shape[0]
    if exact:
        high, low = split(jnp.concatenate([real, imag], axis=0))
        both = dot(matrix[0], jnp.concatenate([high, low], axis=1))
        stacked = both[:, :size] + both[:, size:] + dot(matrix[1], high)
        return stacked[:size], stacked[size:]
    real, imag = real.astype(jnp.bfloat16), imag.astype(jnp.bfloat16)
    columns = jnp.concatenate(
        [jnp.concatenate([real, imag], axis=1), jnp.concatenate([imag, -real], axis=1)], axis=0
    )
    both = dot(matrix[0][:size], columns)
    return both[:, :size], both[:, size:]


def from_right(real, imag, matrix, exact):
    size = real.shape[0]
    stacked = jnp.concatenate([real, imag], axis=1).astype(jnp.bfloat16)
    if exact:
        product = dot(stacked, matrix[0]) + dot(stacked, matrix[1])
    else:
        halves = stacked[: size // 2], stacked[size // 2 :]
        product = jnp.concatenate([dot(half, matrix[0]) for half in halves], axis=0)
    return product[:, :size], product[:, size:]


def wave_kernel(order, incident, turn, upper, measured, *refs):
    depths = len(order)
    matrices, refs, (layers, waves) = refs[:4], refs[4:-2], refs[-2:]
    arrived, outs = refs[: depths + EARLY], refs[depths + EARLY :]
    window = incident.shape[1]
    ahead = [matrices[0][...], matrices[1][...]]
    back = [matrices[2][...], matrices[3][...]]
    depth = lax.axis_index("depth")

    def transform(value, exact):
        return from_right(*from_left(*value, ahead, exact), back, exact)

    def inverse(value, exact):
        return from_right(*from_left(*value, back, exact), ahead, exact)

    above = upper[...] != 0.0
    for place, mask in enumerate(order):
        index = depth ^ mask
        if place < EARLY:
            edge_rows, own_rows = (arrived[p][...].astype(jnp.float32) for p in (place, EARLY + place))
            layers[index, :, :BAND] = jnp.where(above, edge_rows, own_rows)
            layers[index, :, BAND:] = jnp.where(above, own_rows, edge_rows)
        else:
            layers[index] = arrived[EARLY + place][...].astype(jnp.float32)
    real, imag = incident[0], incident[1]
    cosine, sine = turn[0], turn[1]
    scale = 1.0 / window
    for index in range(depths):
        waves[index, 0], waves[index, 1] = real, imag
        layer_real, layer_imag = layers[index, 0], layers[index, 1]
        mixed = (real * layer_real - imag * layer_imag, real * layer_imag + imag * layer_real)
        real, imag = transform(mixed, True)
        if index + 1 < depths:
            turned = (real * cosine - imag * sine, imag * cosine + real * sine)
            real, imag = inverse(turned, True)
    real, imag = real * scale, imag * scale
    misfit = (real * real + imag * imag - measured[depth]) * scale
    adjoint = inverse((misfit * real, misfit * imag), False)
    for index in reversed(range(depths)):
        adj_real, adj_imag = adjoint
        held_real, held_imag = waves[index, 0], waves[index, 1]
        waves[index, 0] = held_real * adj_real + held_imag * adj_imag
        waves[index, 1] = held_real * adj_imag - held_imag * adj_real
        if index > 0:
            layer_real, layer_imag = layers[index, 0], layers[index, 1]
            real, imag = transform(
                (layer_real * adj_real + layer_imag * adj_imag, layer_real * adj_imag - layer_imag * adj_real),
                False,
            )
            adjoint = inverse((real * cosine + imag * sine, imag * cosine - real * sine), False)
    for place, mask in enumerate(order):
        index = depth ^ mask
        if place < LATE:
            first, second = waves[index, :, :BAND], waves[index, :, BAND:]
            outs[place][...] = jnp.where(above, first, second).astype(jnp.bfloat16)
            outs[LATE + place][...] = jnp.where(above, second, first).astype(jnp.bfloat16)
        else:
            outs[LATE + place][...] = waves[index].astype(jnp.bfloat16)


def added(wide, part, block, rows, value, offset, lane):
    value = pltpu.roll(value, offset, 1)
    wide[part, block, rows] += jnp.where(lane >= offset, value, 0.0)
    wide[part, block + 1, rows] += jnp.where(lane < offset, value, 0.0)


def shed_kernel(strip, codes, *refs):
    arrived, (outer, inner, wide) = refs[:-3], refs[-3:]
    columns = outer.shape[3]
    odd = lax.rem(lax.axis_index("tile"), 2)
    wide[:, :, :BAND] = jnp.zeros_like(wide[:, :, :BAND])
    wide[:, :, BAND + strip :] = jnp.zeros_like(wide[:, :, :BAND])
    lane = lax.broadcasted_iota(jnp.int32, (BAND, LANES), 1)
    for place, value in enumerate(arrived):
        row, block, offset = placed(codes, place)
        half, start = edge_half(row, strip)
        half = pl.multiple_of(half, BAND)
        for part in range(2):
            piece = value[part] if value.shape[1] == BAND else value[part, pl.ds(half, BAND)]
            piece = piece.astype(jnp.float32)
            added(wide, part, block, pl.ds(start, BAND), piece, offset, lane)
    far = pl.multiple_of(odd * (strip + BAND), BAND)
    near = pl.multiple_of((1 - odd) * (strip + BAND), BAND)
    for block in range(columns // LANES):
        cols = slice(block * LANES, (block + 1) * LANES)
        for part in range(2):
            outer[part, 0, :, cols] = wide[part, block, pl.ds(far, BAND)].astype(jnp.bfloat16)
            inner[part, 0, :, cols] = wide[part, block, pl.ds(near, BAND)].astype(jnp.bfloat16)


def add_kernel(codes, *refs):
    arrived, (own, wide) = refs[:-2], refs[-2:]
    strip, columns = own.shape[2:]
    window = arrived[-1].shape[1]
    count = len(arrived) - codes.shape[0]
    wide[...] = jnp.zeros_like(wide)
    lane = lax.broadcasted_iota(jnp.int32, (window, LANES), 1)
    for place, value in enumerate(arrived):
        length = value.shape[1]
        row, block, offset = placed(codes, place % count if place < 2 * count else place - count)
        if place < 2 * count:
            half, _ = edge_half(row, strip)
            row += half if place < count else window - BAND - half
        for part in range(2):
            added(wide, part, block, pl.ds(row, length), value[part].astype(jnp.float32), offset, lane[:length])
    for block in range(columns // LANES):
        for part in range(2):
            own[part, 0, :, block * LANES : (block + 1) * LANES] = wide[part, block, BAND : BAND + strip]


def edge_kernel(side, own, band, *refs):
    out, summed, sem = refs[-3:]
    odd = lax.rem(lax.axis_index("tile"), 2)
    rows = pl.ds(pl.multiple_of((odd if side == 0 else 1 - odd) * (own.shape[2] - BAND), BAND), BAND)
    summed[...] = own[:, :, rows] + band[...].astype(jnp.float32)
    copy = pltpu.make_async_copy(summed, out.at[:, :, rows], sem)
    copy.start()
    copy.wait()


def edge(side, own, band, *partial):
    return pl.pallas_call(
        lambda *refs: edge_kernel(side, *refs),
        out_shape=jax.ShapeDtypeStruct(own.shape, own.dtype),
        in_specs=[VMEM, VMEM] + [HBM] * len(partial),
        out_specs=HBM,
        scratch_shapes=[pltpu.VMEM(band.shape, own.dtype), pltpu.SemaphoreType.DMA],
        input_output_aliases={2: 0} if partial else {},
        compiler_params=PARAMS,
    )(own, band, *partial)


def call(kernel, outs, operands, scratch=(), scalars=0):
    return pl.pallas_call(
        kernel,
        out_shape=outs,
        in_specs=[SMEM] * scalars + [VMEM] * (len(operands) - scalars),
        out_specs=jax.tree.map(lambda _: VMEM, outs),
        scratch_shapes=list(scratch),
        compiler_params=PARAMS,
    )(*operands)


def shards(transmission, probe_wave, fresnel_phase, measured, positions, extents):
    tiles, depths = lax.axis_size("tile"), lax.axis_size("depth")
    strip, columns = transmission.shape[2:]
    window = probe_wave.shape[1]
    assert positions.shape[0] == depths == 4 and transmission.shape[1] == 1 and tiles % 2 == 0
    assert strip == 2 * BAND == window
    order = ORDER
    wide = [pltpu.VMEM((2, columns // LANES + 1, strip + 2 * BAND, LANES), jnp.float32)]
    patch = jax.ShapeDtypeStruct((2, window, window), jnp.bfloat16)
    band = jax.ShapeDtypeStruct((2, 1, BAND, columns), jnp.bfloat16)

    piece = jax.ShapeDtypeStruct((2, BAND, window), jnp.bfloat16)

    def swap(value, mask):
        if not mask:
            return value
        return lax.ppermute(value, "depth", [(d, d ^ mask) for d in range(depths)])

    def swapped(values):
        return [swap(v, mask) for v, mask in zip(values, order)]

    def outward(value):
        return lax.ppermute(value, "tile", [(t, (t - 1 + 2 * (t % 2)) % tiles) for t in range(tiles)])

    def inward(value):
        return lax.ppermute(value, "tile", [(t, t ^ 1) for t in range(tiles)])

    places = jax.ShapeDtypeStruct((depths, LANES), jnp.int32)
    total = jax.ShapeDtypeStruct(transmission.shape, jnp.float32)
    own, outer, inner, codes = pl.pallas_call(
        lambda *refs: band_kernel(order, tiles, *refs),
        out_shape=[total, band, band, places],
        in_specs=[HBM, HBM],
        out_specs=[VMEM] * 4,
        scratch_shapes=[pltpu.SMEM((2, depths), jnp.int32), pltpu.SemaphoreType.DMA((3,))],
        compiler_params=PARAMS,
        name="bands",
    )(*(pltpu.with_memory_space_constraint(v, pltpu.HBM) for v in (positions.T, transmission)))
    outer, inner = outward(outer), inward(inner)
    square = jax.ShapeDtypeStruct((2, window, window), jnp.float32)
    full = jax.ShapeDtypeStruct((depths, 2, window, window), jnp.float32)
    windows, *early = call(cut_kernel, [full] + [piece] * EARLY, [codes, own], wide)
    early = swapped(early)
    windows = call(
        lambda *refs: join_kernel(strip, *refs),
        [piece] * EARLY + [patch] * (depths - EARLY),
        [codes, windows, outer, inner],
        wide,
    )
    probe_wave, fresnel_phase, windows = lax.optimization_barrier((probe_wave, fresnel_phase, windows))
    incident, turn, upper = call(
        lambda *refs: prep_kernel(strip, *refs),
        [square, square, jax.ShapeDtypeStruct((BAND, window), jnp.float32)],
        [extents, codes, probe_wave, fresnel_phase],
        scalars=1,
    )
    windows = swapped(windows)
    pieces = call(
        lambda *refs: wave_kernel(order, *refs),
        [piece] * (2 * LATE) + [patch] * (depths - LATE),
        [
            incident,
            turn,
            upper,
            measured,
            *map(jnp.asarray, tables(window)),
            *windows[:EARLY],
            *early,
            *windows[EARLY:],
        ],
        [pltpu.VMEM((depths, 2, window, window), jnp.float32)] * 2,
    )
    late = swapped(pieces[LATE : 2 * LATE])
    pieces = swapped([*pieces[:LATE], *pieces[2 * LATE :]])
    outer, inner = call(lambda *refs: shed_kernel(strip, *refs), [band] * 2, [codes, *pieces], wide)
    outer, inner = outward(outer), inward(inner)
    own = call(add_kernel, total, [codes, *pieces[:LATE], *late, *pieces[LATE:]], wide)
    return edge(0, own, outer, edge(1, own, inner))


def solution(mesh):
    placed = (
        P(None, "depth", "tile", None),
        P(),
        P(),
        P("tile", None, None),
        P("tile", None),
        P("tile", None),
    )
    return jax.shard_map(
        shards,
        mesh=mesh,
        in_specs=placed,
        out_specs=P(None, "depth", "tile", None),
        check_vma=False,
    )
```

```python
import math

import jax
import jax.numpy as jnp
import numpy as np
from jax import lax
from jax.experimental import pallas as pl
from jax.experimental.pallas import tpu as pltpu
from jax.sharding import PartitionSpec as P

BAND = 64
LANES = 128
SPAN = 1 << 16
ORDER = (2, 3, 1, 0)
EARLY = 3
LATE = 3


SMEM = pl.BlockSpec(memory_space=pltpu.SMEM)
VMEM = pl.BlockSpec(memory_space=pltpu.VMEM)
HBM = pl.BlockSpec(memory_space=pltpu.HBM)
PARAMS = pltpu.CompilerParams(vmem_limit_bytes=12 << 20)


def tables(length):
    indices = np.arange(length)
    angles = (indices[:, None] * indices[None, :] % length) * (2.0 * math.pi / length)
    cosine, sine = np.cos(angles), np.sin(angles)
    ahead = np.block([[cosine, sine], [-sine, cosine]]).astype(np.float32)
    back = np.block([[cosine, -sine], [sine, cosine]]).astype(np.float32)
    found = []
    for matrix in (ahead, back):
        high = matrix.astype(jnp.bfloat16)
        found += [high, (matrix - high.astype(np.float32)).astype(jnp.bfloat16)]
    return found


def first_row(positions, probe, tile, strip, tiles):
    rows = strip * tiles
    start = positions[0, probe] - tile * strip + BAND
    start = jnp.where(start < 0, start + rows, start)
    return jnp.where(start >= rows, start - rows, start)


def placed(codes, place):
    code = codes[place : place + 1, :1][0, 0]
    row = lax.div(code, SPAN)
    column = code - row * SPAN
    block = lax.div(column, LANES)
    return row, block, column - block * LANES


def edge_half(row, strip):
    upper = row < BAND
    return jnp.where(upper, 0, BAND), jnp.where(upper, row, row + strip - BAND)


def turned_pair(wide, part, block, rows, offset, lane):
    turn = lax.rem(LANES - offset, LANES)
    left = pltpu.roll(wide[part, block, rows], turn, 1)
    right = pltpu.roll(wide[part, block + 1, rows], turn, 1)
    return jnp.where(lane < LANES - offset, left, right)


def band_kernel(order, tiles, positions_in, own, strip_out, outer, inner, codes, positions, sems):
    strip = strip_out.shape[2]
    tile, depth = lax.axis_index("tile"), lax.axis_index("depth")
    odd = lax.rem(tile, 2)
    outs, copies = (outer, inner), []
    fetch = pltpu.make_async_copy(positions_in, positions, sems.at[2])
    fetch.start()
    for index, side in enumerate((odd, 1 - odd)):
        rows = pl.ds(pl.multiple_of(side * (strip - BAND), BAND), BAND)
        copies.append(pltpu.make_async_copy(own.at[:, :, rows], strip_out.at[:, :, rows], sems.at[index]))
        copies[-1].start()
    fetch.wait()
    for place, mask in enumerate(order):
        probe = depth ^ mask
        row = first_row(positions, probe, tile, strip, tiles)
        codes[place : place + 1] = jnp.full((1, LANES), row * SPAN + positions[1, probe], jnp.int32)
    for copy, side, out in zip(copies, (odd, 1 - odd), outs):
        copy.wait()
        rows = pl.ds(pl.multiple_of(side * (strip - BAND), BAND), BAND)
        out[...] = strip_out[:, :, rows].astype(jnp.bfloat16)


def cut_kernel(codes, own, out, *refs):
    early, wide = refs[:-1], refs[-1]
    strip, columns = own.shape[2:]
    window = out.shape[2]
    for block in range(columns // LANES):
        for part in range(2):
            wide[part, block, BAND : BAND + strip] = own[part, 0, :, block * LANES : (block + 1) * LANES]
    lane = lax.broadcasted_iota(jnp.int32, (window, LANES), 1)
    for place in range(out.shape[0]):
        row, block, offset = placed(codes, place)
        for part in range(2):
            out[place, part] = turned_pair(wide, part, block, pl.ds(row, window), offset, lane)
        if place < len(early):
            half, _ = edge_half(row, strip)
            other = pl.multiple_of(window - BAND - half, BAND)
            early[place][...] = out[place, :, pl.ds(other, BAND)].astype(jnp.bfloat16)


def prep_kernel(strip, extents, codes, probe_wave, fresnel_phase, incident, turn, upper):
    window = probe_wave.shape[1]
    row, _, _ = placed(codes, codes.shape[0] - 1)
    line = row - BAND + lax.broadcasted_iota(jnp.int32, (window, window), 0)
    inside = (line >= -extents[0, 0]) & (line < strip + extents[0, 1])
    for part in range(2):
        incident[part] = jnp.where(inside, probe_wave[part], 0.0)
    upper[...] = jnp.full(upper.shape, row < BAND).astype(jnp.float32).astype(upper.dtype)
    scale = 1.0 / window**2
    turn[0] = jnp.cos(fresnel_phase[...]) * scale
    turn[1] = jnp.sin(fresnel_phase[...]) * scale


def join_kernel(strip, codes, windows, outer, inner, *refs):
    outs, wide = refs[:-1], refs[-1]
    columns = outer.shape[3]
    window = windows.shape[2]
    odd = lax.rem(lax.axis_index("tile"), 2)
    for block in range(columns // LANES):
        cols = slice(block * LANES, (block + 1) * LANES)
        for part in range(2):
            far = pl.multiple_of(odd * (strip + BAND), BAND)
            near = pl.multiple_of((1 - odd) * (strip + BAND), BAND)
            wide[part, block, pl.ds(far, BAND)] = outer[part, 0, :, cols].astype(jnp.float32)
            wide[part, block, pl.ds(near, BAND)] = inner[part, 0, :, cols].astype(jnp.float32)
    lane = lax.broadcasted_iota(jnp.int32, (BAND, LANES), 1)
    line = lax.broadcasted_iota(jnp.int32, (BAND, LANES), 0)
    for place, out in enumerate(outs):
        row, block, offset = placed(codes, place)
        half, start = edge_half(row, strip)
        within = row + half + line
        outside = (within < BAND) | (within >= BAND + strip)
        half = pl.multiple_of(half, BAND)
        other = pl.multiple_of(window - BAND - half, BAND)
        for part in range(2):
            band = turned_pair(wide, part, block, pl.ds(start, BAND), offset, lane)
            joined = jnp.where(outside, band, windows[place, part, pl.ds(half, BAND)]).astype(jnp.bfloat16)
            if out.shape[1] == BAND:
                out[part] = joined
                continue
            out[part, pl.ds(half, BAND)] = joined
            out[part, pl.ds(other, BAND)] = windows[place, part, pl.ds(other, BAND)].astype(jnp.bfloat16)


def split(value):
    high = value.astype(jnp.bfloat16)
    return high, (value - high.astype(jnp.float32)).astype(jnp.bfloat16)


def dot(left, right):
    return jnp.dot(left, right, preferred_element_type=jnp.float32)


def from_left(real, imag, matrix, exact):
    size = real.shape[0]
    if exact:
        high, low = split(jnp.concatenate([real, imag], axis=0))
        both = dot(matrix[0], jnp.concatenate([high, low], axis=1))
        stacked = both[:, :size] + both[:, size:] + dot(matrix[1], high)
        return stacked[:size], stacked[size:]
    real, imag = real.astype(jnp.bfloat16), imag.astype(jnp.bfloat16)
    columns = jnp.concatenate(
        [jnp.concatenate([real, imag], axis=1), jnp.concatenate([imag, -real], axis=1)], axis=0
    )
    both = dot(matrix[0][:size], columns)
    return both[:, :size], both[:, size:]


def from_right(real, imag, matrix, exact):
    size = real.shape[0]
    stacked = jnp.concatenate([real, imag], axis=1).astype(jnp.bfloat16)
    if exact:
        product = dot(stacked, matrix[0]) + dot(stacked, matrix[1])
    else:
        halves = stacked[: size // 2], stacked[size // 2 :]
        product = jnp.concatenate([dot(half, matrix[0]) for half in halves], axis=0)
    return product[:, :size], product[:, size:]


def wave_kernel(order, incident, turn, upper, measured, *refs):
    depths = len(order)
    matrices, refs, (layers, waves) = refs[:4], refs[4:-2], refs[-2:]
    arrived, outs = refs[: depths + EARLY], refs[depths + EARLY :]
    window = incident.shape[1]
    ahead = [matrices[0][...], matrices[1][...]]
    back = [matrices[2][...], matrices[3][...]]
    depth = lax.axis_index("depth")

    def transform(value, exact):
        return from_right(*from_left(*value, ahead, exact), back, exact)

    def inverse(value, exact):
        return from_right(*from_left(*value, back, exact), ahead, exact)

    above = upper[...] != 0
    above_wide = upper[...].astype(jnp.float32) != 0.0
    for place, mask in enumerate(order):
        index = depth ^ mask
        if place < EARLY:
            edge_rows, own_rows = arrived[place][...], arrived[EARLY + place][...]
            layers[index, :, :BAND] = jnp.where(above, edge_rows, own_rows)
            layers[index, :, BAND:] = jnp.where(above, own_rows, edge_rows)
        else:
            layers[index] = arrived[EARLY + place][...]
    real, imag = incident[0], incident[1]
    cosine, sine = turn[0], turn[1]
    scale = 1.0 / window
    for index in range(depths):
        waves[index, 0], waves[index, 1] = real, imag
        layer_real, layer_imag = layers[index, 0].astype(jnp.float32), layers[index, 1].astype(jnp.float32)
        mixed = (real * layer_real - imag * layer_imag, real * layer_imag + imag * layer_real)
        real, imag = transform(mixed, True)
        if index + 1 < depths:
            turned = (real * cosine - imag * sine, imag * cosine + real * sine)
            real, imag = inverse(turned, True)
    real, imag = real * scale, imag * scale
    misfit = (real * real + imag * imag - measured[depth]) * scale
    adjoint = inverse((misfit * real, misfit * imag), False)
    for index in reversed(range(depths)):
        adj_real, adj_imag = adjoint
        held_real, held_imag = waves[index, 0], waves[index, 1]
        waves[index, 0] = held_real * adj_real + held_imag * adj_imag
        waves[index, 1] = held_real * adj_imag - held_imag * adj_real
        if index > 0:
            layer_real, layer_imag = layers[index, 0].astype(jnp.float32), layers[index, 1].astype(jnp.float32)
            real, imag = transform(
                (layer_real * adj_real + layer_imag * adj_imag, layer_real * adj_imag - layer_imag * adj_real),
                False,
            )
            adjoint = inverse((real * cosine + imag * sine, imag * cosine - real * sine), False)
    for place, mask in enumerate(order):
        index = depth ^ mask
        if place < LATE:
            first, second = waves[index, :, :BAND], waves[index, :, BAND:]
            outs[place][...] = jnp.where(above_wide, first, second).astype(jnp.bfloat16)
            outs[LATE + place][...] = jnp.where(above_wide, second, first).astype(jnp.bfloat16)
        else:
            outs[LATE + place][...] = waves[index].astype(jnp.bfloat16)


def added(wide, part, block, rows, value, offset, lane):
    value = pltpu.roll(value, offset, 1)
    wide[part, block, rows] += jnp.where(lane >= offset, value, 0.0)
    wide[part, block + 1, rows] += jnp.where(lane < offset, value, 0.0)


def shed_kernel(strip, codes, *refs):
    arrived, (outer, inner, wide) = refs[:-3], refs[-3:]
    columns = outer.shape[3]
    odd = lax.rem(lax.axis_index("tile"), 2)
    wide[:, :, :BAND] = jnp.zeros_like(wide[:, :, :BAND])
    wide[:, :, BAND + strip :] = jnp.zeros_like(wide[:, :, :BAND])
    lane = lax.broadcasted_iota(jnp.int32, (BAND, LANES), 1)
    for place, value in enumerate(arrived):
        row, block, offset = placed(codes, place)
        half, start = edge_half(row, strip)
        half = pl.multiple_of(half, BAND)
        for part in range(2):
            piece = value[part] if value.shape[1] == BAND else value[part, pl.ds(half, BAND)]
            piece = piece.astype(jnp.float32)
            added(wide, part, block, pl.ds(start, BAND), piece, offset, lane)
    far = pl.multiple_of(odd * (strip + BAND), BAND)
    near = pl.multiple_of((1 - odd) * (strip + BAND), BAND)
    for block in range(columns // LANES):
        cols = slice(block * LANES, (block + 1) * LANES)
        for part in range(2):
            outer[part, 0, :, cols] = wide[part, block, pl.ds(far, BAND)].astype(jnp.bfloat16)
            inner[part, 0, :, cols] = wide[part, block, pl.ds(near, BAND)].astype(jnp.bfloat16)


def add_kernel(codes, *refs):
    arrived, (own, wide) = refs[:-2], refs[-2:]
    strip, columns = own.shape[2:]
    window = arrived[-1].shape[1]
    count = len(arrived) - codes.shape[0]
    wide[...] = jnp.zeros_like(wide)
    lane = lax.broadcasted_iota(jnp.int32, (window, LANES), 1)
    for place, value in enumerate(arrived):
        length = value.shape[1]
        row, block, offset = placed(codes, place % count if place < 2 * count else place - count)
        if place < 2 * count:
            half, _ = edge_half(row, strip)
            row += half if place < count else window - BAND - half
        for part in range(2):
            added(wide, part, block, pl.ds(row, length), value[part].astype(jnp.float32), offset, lane[:length])
    for block in range(columns // LANES):
        for part in range(2):
            own[part, 0, :, block * LANES : (block + 1) * LANES] = wide[part, block, BAND : BAND + strip]


def edge_kernel(side, own, band, *refs):
    out, summed, sem = refs[-3:]
    odd = lax.rem(lax.axis_index("tile"), 2)
    rows = pl.ds(pl.multiple_of((odd if side == 0 else 1 - odd) * (own.shape[2] - BAND), BAND), BAND)
    summed[...] = own[:, :, rows] + band[...].astype(jnp.float32)
    copy = pltpu.make_async_copy(summed, out.at[:, :, rows], sem)
    copy.start()
    copy.wait()


def edge(side, own, band, *partial):
    return pl.pallas_call(
        lambda *refs: edge_kernel(side, *refs),
        out_shape=jax.ShapeDtypeStruct(own.shape, own.dtype),
        in_specs=[VMEM, VMEM] + [HBM] * len(partial),
        out_specs=HBM,
        scratch_shapes=[pltpu.VMEM(band.shape, own.dtype), pltpu.SemaphoreType.DMA],
        input_output_aliases={2: 0} if partial else {},
        compiler_params=PARAMS,
    )(own, band, *partial)


def call(kernel, outs, operands, scratch=(), scalars=0):
    return pl.pallas_call(
        kernel,
        out_shape=outs,
        in_specs=[SMEM] * scalars + [VMEM] * (len(operands) - scalars),
        out_specs=jax.tree.map(lambda _: VMEM, outs),
        scratch_shapes=list(scratch),
        compiler_params=PARAMS,
    )(*operands)


def shards(transmission, probe_wave, fresnel_phase, measured, positions, extents):
    tiles, depths = lax.axis_size("tile"), lax.axis_size("depth")
    strip, columns = transmission.shape[2:]
    window = probe_wave.shape[1]
    assert positions.shape[0] == depths == 4 and transmission.shape[1] == 1 and tiles % 2 == 0
    assert strip == 2 * BAND == window
    order = ORDER
    wide = [pltpu.VMEM((2, columns // LANES + 1, strip + 2 * BAND, LANES), jnp.float32)]
    patch = jax.ShapeDtypeStruct((2, window, window), jnp.bfloat16)
    band = jax.ShapeDtypeStruct((2, 1, BAND, columns), jnp.bfloat16)

    piece = jax.ShapeDtypeStruct((2, BAND, window), jnp.bfloat16)

    def swap(value, mask):
        if not mask:
            return value
        return lax.ppermute(value, "depth", [(d, d ^ mask) for d in range(depths)])

    def swapped(values):
        return [swap(v, mask) for v, mask in zip(values, order)]

    def outward(value):
        return lax.ppermute(value, "tile", [(t, (t - 1 + 2 * (t % 2)) % tiles) for t in range(tiles)])

    def inward(value):
        return lax.ppermute(value, "tile", [(t, t ^ 1) for t in range(tiles)])

    places = jax.ShapeDtypeStruct((depths, LANES), jnp.int32)
    total = jax.ShapeDtypeStruct(transmission.shape, jnp.float32)
    own, outer, inner, codes = pl.pallas_call(
        lambda *refs: band_kernel(order, tiles, *refs),
        out_shape=[total, band, band, places],
        in_specs=[HBM, HBM],
        out_specs=[VMEM] * 4,
        scratch_shapes=[pltpu.SMEM((2, depths), jnp.int32), pltpu.SemaphoreType.DMA((3,))],
        compiler_params=PARAMS,
        name="bands",
    )(*(pltpu.with_memory_space_constraint(v, pltpu.HBM) for v in (positions.T, transmission)))
    outer, inner = outward(outer), inward(inner)
    square = jax.ShapeDtypeStruct((2, window, window), jnp.float32)
    full = jax.ShapeDtypeStruct((depths, 2, window, window), jnp.float32)
    windows, *early = call(cut_kernel, [full] + [piece] * EARLY, [codes, own], wide)
    early = swapped(early)
    windows = call(
        lambda *refs: join_kernel(strip, *refs),
        [piece] * EARLY + [patch] * (depths - EARLY),
        [codes, windows, outer, inner],
        wide,
    )
    probe_wave, fresnel_phase, windows = lax.optimization_barrier((probe_wave, fresnel_phase, windows))
    incident, turn, upper = call(
        lambda *refs: prep_kernel(strip, *refs),
        [square, square, jax.ShapeDtypeStruct((BAND, window), jnp.bfloat16)],
        [extents, codes, probe_wave, fresnel_phase],
        scalars=1,
    )
    windows = swapped(windows)
    pieces = call(
        lambda *refs: wave_kernel(order, *refs),
        [piece] * (2 * LATE) + [patch] * (depths - LATE),
        [
            incident,
            turn,
            upper,
            measured,
            *map(jnp.asarray, tables(window)),
            *windows[:EARLY],
            *early,
            *windows[EARLY:],
        ],
        [pltpu.VMEM((depths, 2, window, window), kind) for kind in (jnp.bfloat16, jnp.float32)],
    )
    late = swapped(pieces[LATE : 2 * LATE])
    pieces = swapped([*pieces[:LATE], *pieces[2 * LATE :]])
    outer, inner = call(lambda *refs: shed_kernel(strip, *refs), [band] * 2, [codes, *pieces], wide)
    outer, inner = outward(outer), inward(inner)
    own = call(add_kernel, total, [codes, *pieces[:LATE], *late, *pieces[LATE:]], wide)
    return edge(0, own, outer, edge(1, own, inner))


def solution(mesh):
    placed = (
        P(None, "depth", "tile", None),
        P(),
        P(),
        P("tile", None, None),
        P("tile", None),
        P("tile", None),
    )
    return jax.shard_map(
        shards,
        mesh=mesh,
        in_specs=placed,
        out_specs=P(None, "depth", "tile", None),
        check_vma=False,
    )
```
